128 devices in a mesh: gx: 8 (over z, core), gy: 16 (over x, y).
Axes of the slice: x: 4, y: 4, z: 4, core: 2. Of those that a mesh axis runs over, the one named last changes fastest.
Arguments:
- hidden_in: bfloat16 [128, 8192], P(('gx', 'gy')), may hold values from -6 to 6
- norm_gain: float32 [8192], replicated, may hold values from 0.5 to 1.5
- w_query: bfloat16 [8192, 8192], P('gx', 'gy'), may hold values from -0.0625 to 0.0625
- key_weight: bfloat16 [8192, 1024], P('gx', 'gy'), may hold values from -0.375 to 0.375
- value_weight: bfloat16 [8192, 1024], P('gx', 'gy'), may hold values from -0.0625 to 0.0625
- w_output: bfloat16 [8192, 8192], P('gx', 'gy'), may hold values from -0.0625 to 0.0625
- key_cache_units: bfloat16 [128, 2048, 1024], P(('gx', 'gy')), may hold values from -6 to 6
- value_cache_units: bfloat16 [128, 2048, 1024], P(('gx', 'gy')), may hold values from -6 to 6
- key_scale: float32 [128, 16, 8], P(('gx', 'gy')), may hold values from 0.5 to 40
- value_block_scale: float32 [128, 16, 8], P(('gx', 'gy')), may hold values from 0.5 to 2
- lengths: int32 [128], P(('gx', 'gy')), may hold values from 256 to 2048, as said below
Outputs:
- hidden_out: bfloat16 [128, 8192], P(('gx', 'gy'))
The draws below stay inside these ranges and needn't reach their ends.
Inputs may be any that keep to these rules, and one draw needn't show every extreme that they name: Request r has lengths[r] cached tokens at positions 0 to lengths[r] - 1 of its cache, the new token stands at position lengths[r]; some request has exactly 2048 and some exactly 256.
All inputs are finite; a program needn't handle non-finite values.
Results may differ from the reference program's by a relative error of at most 0.008.
The reference program's roundings to bfloat16 on the way count: a program that leaves them out, or rounds other values in their place, can miss the bound.
Values may be sent and summed in bfloat16 or wider, within the bound.
A program may use at most 64 MiB of HBM per device.

```python
import math
import jax
import jax.numpy as jnp
from jax import lax

MODEL_WIDTH = 8192
HQ = 64
KEY_VALUE_HEADS = 8
HEAD_SIZE = 128
CACHE_SLOTS = 2048
SCALE_BLOCK = 128
REQUEST_COUNT = 128


def draw_key_scale(key, part):
    key_base = jax.random.fold_in(key, 0)
    scale_layout = (REQUEST_COUNT, CACHE_SLOTS // SCALE_BLOCK, KEY_VALUE_HEADS)
    scales = jnp.exp(jax.random.uniform(key_base, scale_layout, jnp.float32, math.log(0.5), math.log(5.0)))
    return scales


def draw_lengths(key, part):
    key_vals, key_long, key_short = jax.random.split(key, 3)
    sampled = jax.random.randint(key_vals, (REQUEST_COUNT,), CACHE_SLOTS // 8, CACHE_SLOTS + 1)
    long_place = jax.random.randint(key_long, (), 0, REQUEST_COUNT)
    short_step = jax.random.randint(key_short, (), 1, REQUEST_COUNT)
    short_place = (long_place + short_step) % REQUEST_COUNT
    sampled = sampled.at[long_place].set(CACHE_SLOTS)
    return sampled.at[short_place].set(CACHE_SLOTS // 8)


def level_of(stream_key, shape, cuts, least, top_value):
    level, own = 1.0, jax.random.fold_in(stream_key, 6)
    for dim, parts in cuts:
        heights = jnp.exp(jax.random.uniform(jax.random.fold_in(own, dim), (parts,), jnp.float32, least / len(cuts), top_value / len(cuts)))
        level = level * jnp.repeat(heights, shape[dim] // parts).reshape([-1 if axis == dim else 1 for axis in range(len(shape))])
    return level


def gaussian(own_key, extent, scale, bound, cuts=(), kind=jnp.bfloat16):
    drawn = jax.random.normal(own_key, extent, jnp.float32) * scale
    if len(cuts) > 0:
        drawn = level_of(own_key, extent, cuts, -0.22, 0.18) * drawn
    return jnp.clip(drawn, min=-bound, max=bound).astype(kind)


def setup_inputs(seed: int = 0) -> dict:
    seeds = jax.random.split(jax.random.key(seed), 12)
    hidden_in = gaussian(seeds[0], (REQUEST_COUNT, MODEL_WIDTH), 1.0, 6.0, ((0, 128),))
    norm_gain = jnp.clip(1.0 + 0.1 * jax.random.normal(seeds[1], (MODEL_WIDTH,), jnp.float32), 0.5, 1.5)
    w_query = gaussian(seeds[2], (MODEL_WIDTH, HQ * HEAD_SIZE), MODEL_WIDTH ** -0.5, 0.0625, ((0, 8), (1, 16)))
    key_weight = gaussian(seeds[3], (MODEL_WIDTH, KEY_VALUE_HEADS * HEAD_SIZE), (MODEL_WIDTH // 32) ** -0.5, 0.375, ((0, 8), (1, 16)))
    value_weight = gaussian(seeds[4], (MODEL_WIDTH, KEY_VALUE_HEADS * HEAD_SIZE), MODEL_WIDTH ** -0.5, 0.0625, ((0, 8), (1, 16)))
    w_output = gaussian(seeds[5], (HQ * HEAD_SIZE, MODEL_WIDTH), (HQ * HEAD_SIZE) ** -0.5, 0.0625, ((0, 8), (1, 16)))
    key_cache_units = gaussian(seeds[6], (REQUEST_COUNT, CACHE_SLOTS, KEY_VALUE_HEADS * HEAD_SIZE), 1.0, 6.0, ((0, 128),))
    value_cache_units = gaussian(seeds[7], (REQUEST_COUNT, CACHE_SLOTS, KEY_VALUE_HEADS * HEAD_SIZE), 1.0, 6.0, ((0, 128),))
    key_scale = draw_key_scale(jax.random.fold_in(seeds[11], 71), 0)
    value_block_scale = jnp.clip(jnp.exp(math.log(2.0) - 1.3862944 * jax.random.uniform(seeds[9], (REQUEST_COUNT, CACHE_SLOTS // SCALE_BLOCK, KEY_VALUE_HEADS), jnp.float32) ** level_of(seeds[9], (REQUEST_COUNT, CACHE_SLOTS // SCALE_BLOCK, KEY_VALUE_HEADS), ((0, 128),), -0.2, 0.2)), 0.5, 2.0)
    lengths = draw_lengths(jax.random.fold_in(seeds[11], 71), 0)
    return dict(hidden_in=hidden_in, norm_gain=norm_gain, w_query=w_query, key_weight=key_weight, value_weight=value_weight, w_output=w_output, key_cache_units=key_cache_units, value_cache_units=value_cache_units, key_scale=key_scale, value_block_scale=value_block_scale, lengths=lengths)


ROPE_BASE = 500000.0
NORM_EPS = 1e-05
MASKED_SCORE = -1e+30

def apply_rotary(values, positions):
    head_dim = values.shape[-1]
    half_dim = head_dim // 2
    freqs = ROPE_BASE ** (-(jnp.arange(half_dim, dtype=jnp.float32) * 2.0) / head_dim)
    angles = positions.astype(jnp.float32)[:, None, None] * freqs
    cosine = jnp.cos(angles)
    sine = jnp.sin(angles)
    wide_vals = values.astype(jnp.float32)
    front_half = wide_vals[..., :half_dim]
    back_half = wide_vals[..., half_dim:]
    joined = jnp.concatenate([front_half * cosine - back_half * sine, back_half * cosine + front_half * sine], axis=-1)
    return joined.astype(jnp.bfloat16)

def attend_exact(query, new_key, new_value, keys, values, key_scale, value_block_scale, length):
    heads, head_dim = query.shape
    kv_heads = new_key.shape[0]
    capacity = keys.shape[0]
    group_size = heads // kv_heads
    blocks = key_scale.shape[0]
    inv_root = 1.0 / math.sqrt(head_dim)
    grouped = query.reshape(kv_heads, group_size, head_dim).astype(jnp.float32)
    key_rows = keys.reshape(capacity, kv_heads, head_dim).astype(jnp.float32)
    value_rows = values.reshape(capacity, kv_heads, head_dim).astype(jnp.float32)
    raw_scores = jnp.einsum('gqd,tgd->gqt', grouped, key_rows)
    scaled = raw_scores.reshape(kv_heads, group_size, blocks, capacity // blocks) * key_scale.T[:, None, :, None]
    scores = scaled.reshape(kv_heads, group_size, capacity) * inv_root
    live_mask = jnp.arange(capacity) < length
    scores = jnp.where(live_mask, scores, MASKED_SCORE)
    own_score = jnp.einsum('gqd,gd->gq', grouped, new_key.astype(jnp.float32)) * inv_root
    peak_score = jnp.maximum(lax.optimization_barrier(jnp.max(scores, axis=-1)), own_score)
    probs = jnp.where(live_mask, jnp.exp(scores - peak_score[..., None]), 0.0)
    own_prob = jnp.exp(own_score - peak_score)
    total_weight = lax.optimization_barrier(jnp.sum(probs, axis=-1)) + own_prob
    scaled_probs = probs.reshape(kv_heads, group_size, blocks, capacity // blocks) * value_block_scale.T[:, None, :, None]
    weighted = lax.optimization_barrier(scaled_probs.reshape(kv_heads, group_size, capacity).astype(jnp.bfloat16)).astype(jnp.float32)
    own_weight = lax.optimization_barrier(own_prob.astype(jnp.bfloat16)).astype(jnp.float32)
    summed = jnp.einsum('gqt,tgd->gqd', weighted, value_rows)
    summed = summed + own_weight[..., None] * new_value.astype(jnp.float32)[:, None, :]
    return (summed / total_weight[..., None]).astype(jnp.bfloat16).reshape(heads * head_dim)

def reference(hidden_in, norm_gain, w_query, key_weight, value_weight, w_output, key_cache_units, value_cache_units, key_scale, value_block_scale, lengths):
    wide_input = hidden_in.astype(jnp.float32)
    variance = lax.optimization_barrier(jnp.mean(wide_input * wide_input, axis=1, keepdims=True))
    normed = (wide_input * lax.rsqrt(variance + NORM_EPS) * norm_gain).astype(jnp.bfloat16)
    query_proj = jnp.dot(normed, w_query, preferred_element_type=jnp.float32).astype(jnp.bfloat16)
    key_projected = jnp.dot(normed, key_weight, preferred_element_type=jnp.float32).astype(jnp.bfloat16)
    value_projected = jnp.dot(normed, value_weight, preferred_element_type=jnp.float32).astype(jnp.bfloat16)
    query_rot = apply_rotary(query_proj.reshape(REQUEST_COUNT, HQ, HEAD_SIZE), lengths)
    key_rotated = apply_rotary(key_projected.reshape(REQUEST_COUNT, KEY_VALUE_HEADS, HEAD_SIZE), lengths)
    fresh_value = value_projected.reshape(REQUEST_COUNT, KEY_VALUE_HEADS, HEAD_SIZE)
    attended = lax.map(lambda items: attend_exact(*items), (query_rot, key_rotated, fresh_value, key_cache_units, value_cache_units, key_scale, value_block_scale, lengths))
    update = jnp.dot(attended, w_output, preferred_element_type=jnp.float32)
    return (wide_input + update).astype(jnp.bfloat16)
```

```python
import functools
import math

import jax
import jax.numpy as jnp
from jax import lax
from jax.experimental import pallas as pl
from jax.experimental.pallas import tpu as pltpu
from jax.sharding import PartitionSpec as P

MESH = pl.DeviceIdType.MESH
F32 = jnp.float32
BF16 = jnp.bfloat16

GROUPS = 8
LANES = 128
ROPE_BASE = 500000.0
NORM_EPS = 1e-05
MASKED_SCORE = -1e30


def kernel(
    nx,
    ny,
    hidden_hbm,
    gain_hbm,
    wq_hbm,
    wk_hbm,
    wv_hbm,
    wo_hbm,
    keys_hbm,
    values_hbm,
    key_scale,
    value_scale,
    lengths,
    out_ref,
    hidden,
    gain,
    wq,
    wk,
    wv,
    wkv,
    wo,
    keys,
    values,
    wide,
    normed,
    a1,
    a2_src,
    a2,
    prod,
    b1_src,
    b1,
    b2_src,
    b2,
    rows,
    queries,
    kscale,
    vscale,
    c_src,
    c1,
    c2_src,
    c2,
    d1_src,
    d1,
    d2_src,
    d2,
    load_sem,
    send_x,
    recv_x,
    send_y,
    recv_y,
):
    gx = lax.axis_index("gx")
    gy = lax.axis_index("gy")
    slots = keys.shape[0]
    blocks = slots // LANES
    key_cols = wk.shape[1]

    loads = [
        pltpu.make_async_copy(src, dst, load_sem.at[i])
        for i, (src, dst) in enumerate(
            (
                (hidden_hbm, hidden),
                (gain_hbm, gain),
                (wk_hbm, wk),
                (wv_hbm, wv),
                (wq_hbm, wq),
                (keys_hbm, keys),
                (values_hbm, values),
                (wo_hbm, wo),
            )
        )
    ]
    for load in loads:
        load.start()

    barrier = pltpu.get_barrier_semaphore()

    @pl.loop(1, nx)
    def _(j):
        pl.semaphore_signal(
            barrier, inc=1, device_id=(lax.rem(gx + j, nx), gy), device_id_type=MESH
        )

    @pl.loop(1, ny)
    def _(j):
        pl.semaphore_signal(
            barrier, inc=1, device_id=(gx, lax.rem(gy + j, ny)), device_id_type=MESH
        )

    def copy_x(stage, src, dst, peer, slot):
        return pltpu.make_async_remote_copy(
            src_ref=src(peer),
            dst_ref=dst(slot),
            send_sem=send_x.at[stage, peer],
            recv_sem=recv_x.at[stage, slot],
            device_id=(peer, gy),
            device_id_type=MESH,
        )

    def copy_y(stage, src, dst, peer, slot):
        return pltpu.make_async_remote_copy(
            src_ref=src(peer),
            dst_ref=dst(slot),
            send_sem=send_y.at[stage, peer],
            recv_sem=recv_y.at[stage, slot],
            device_id=(gx, peer),
            device_id_type=MESH,
        )

    def start_all(copy, n, me, stage, src, dst):
        @pl.loop(1, n)
        def _(j):
            copy(stage, src, dst, lax.rem(me + j, n), me).start()

    def wait_recv(copy, n, me, stage, src, dst):
        @pl.loop(1, n)
        def _(j):
            peer = lax.rem(me + j, n)
            copy(stage, src, dst, peer, peer).wait_recv()

    def wait_send(copy, n, me, stage, src, dst):
        @pl.loop(1, n)
        def _(j):
            copy(stage, src, dst, lax.rem(me + j, n), me).wait_send()

    def tile(ref, count=8):
        return lambda i: ref.at[pl.ds(pl.multiple_of(i * count, count), count)]

    def lead(ref):
        return lambda i: ref.at[i]

    def whole(ref):
        return lambda i: ref

    loads[0].wait()
    row = hidden[...].astype(F32)
    for s in range(wide.shape[0]):
        wide[s : s + 1, :] = row[:, s * LANES : (s + 1) * LANES]
    loads[1].wait()
    x = wide[...]
    variance = jnp.sum(jnp.sum(x * x, axis=0, keepdims=True), axis=1, keepdims=True) * (
        1.0 / (x.shape[0] * LANES)
    )
    normed[...] = (x * lax.rsqrt(variance + NORM_EPS) * gain[...]).astype(BF16).astype(F32)

    pl.semaphore_wait(barrier, nx + ny - 2)

    def spread(stage, src, first, second_src, second):
        start_all(copy_x, nx, gx, stage, tile(src), tile(first))
        own = pl.multiple_of(gx * 8, 8)
        first[pl.ds(own, 8), :] = src[pl.ds(own, 8), :]

    def gather(stage, src, first, second_src, second):
        wait_recv(copy_x, nx, gx, stage, tile(src), tile(first))
        chunks = [first[pl.ds(s, nx, stride=8), :] for s in range(8)]
        halves = jnp.concatenate(
            [jnp.concatenate(chunks[:4], axis=1), jnp.concatenate(chunks[4:], axis=1)], axis=0
        ).astype(BF16)
        second_src[...] = halves
        start_all(copy_y, ny, gy, stage, whole(second_src), lead(second))
        second[gy] = halves

    def gathered(stage, second_src, second):
        wait_recv(copy_y, ny, gy, stage, whole(second_src), lead(second))
        both = second[...].astype(F32)
        count = nx * ny
        width = both.shape[-1]
        return (
            both[:, :8].reshape(count, width).astype(BF16),
            both[:, 8:].reshape(count, width).astype(BF16),
        )

    spread(0, normed, a1, a2_src, a2)

    length = lengths[0]
    lane = lax.broadcasted_iota(jnp.int32, (1, LANES), 1)
    step = (lane % 64).astype(F32)
    angle = length.astype(F32) * jnp.exp(step * (-2.0 * math.log(ROPE_BASE) / LANES))
    cosine = jnp.cos(angle)
    sine = jnp.sin(angle)
    sine = jnp.where(lane < 64, -sine, sine)
    inv_root = 1.0 / math.sqrt(LANES)

    gather(0, normed, a1, a2_src, a2)

    @pl.loop(0, blocks)
    def _(b):
        at = pl.ds(pl.multiple_of(b * LANES, LANES), LANES)
        for g in range(GROUPS):
            kscale[8 * g : 8 * g + 8, at] = jnp.full((8, LANES), key_scale[b, g] * inv_root, F32)
            vscale[8 * g : 8 * g + 8, at] = jnp.full((8, LANES), value_scale[b, g], F32)

    loads[2].wait()
    loads[3].wait()
    wkv[...] = jnp.concatenate([wk[...], wv[...]], axis=1)
    loads[4].wait()

    def matmul(low, high, weights):
        half = weights.shape[0] // 2
        return jnp.dot(low, weights[:half], preferred_element_type=F32) + jnp.dot(
            high, weights[half:], preferred_element_type=F32
        )

    def reduce_start(stage, parts, src, dst):
        at = 0
        for part in parts:
            for c in range(part.shape[1] // LANES):
                prod[at] = part[:, c * LANES : (c + 1) * LANES]
                at += 1
        for target in range(nx):
            for c in range(at):
                src[target, :, c * LANES : (c + 1) * LANES] = prod.at[c][
                    pl.ds(target, ny, stride=nx), :
                ]
        start_all(copy_x, nx, gx, stage, lead(src), lead(dst))
        dst[gx] = src[gx]

    def reduce_end(stage, src, dst):
        wait_recv(copy_x, nx, gx, stage, lead(src), lead(dst))
        total = dst[0]
        for i in range(1, nx):
            total = total + dst[i]
        return total

    def rows_start(stage, summed, src, dst):
        for c in range(summed.shape[1] // LANES):
            src[pl.ds(c, ny, stride=8), :] = summed[:, c * LANES : (c + 1) * LANES]
        start_all(copy_y, ny, gy, stage, tile(src), tile(dst))
        own = pl.multiple_of(gy * 8, 8)
        dst[pl.ds(own, 8), :] = src[pl.ds(own, 8), :]

    low, high = gathered(0, a2_src, a2)
    reduce_start(1, (matmul(low, high, wq), matmul(low, high, wkv)), b1_src, b1)
    b2_src[...] = jnp.zeros_like(b2_src)
    d2_src[...] = jnp.zeros_like(d2_src)
    summed = reduce_end(1, b1_src, b1).astype(BF16).astype(F32)
    rows_start(1, summed, b2_src, b2)
    wait_recv(copy_y, ny, gy, 1, tile(b2_src), tile(b2))

    per = wq.shape[1] // LANES
    for j in range(per):
        rows[pl.ds(j, ny, stride=per), :] = b2[pl.ds(j, ny, stride=8), :]
    even = b2[pl.ds(per, ny // 2, stride=16), :]
    odd = b2[pl.ds(per + 8, ny // 2, stride=16), :]
    front = lane < 64
    new_key = jnp.where(front, even, pltpu.roll(odd, 64, 1))
    new_value = jnp.where(front, pltpu.roll(even, 64, 1), odd)

    def rotate(v):
        return (v * cosine + pltpu.roll(v, 64, 1) * sine).astype(BF16).astype(F32)

    new_key = rotate(new_key)
    queries[...] = rotate(rows[...])

    loads[5].wait()
    loads[6].wait()
    top = lax.broadcasted_iota(jnp.int32, (16, LANES), 0) < 8
    live = lax.broadcasted_iota(jnp.int32, (1, slots), 1) < length
    for p in range(GROUPS // 2):
        cols = slice(2 * p * LANES, 2 * (p + 1) * LANES)
        heads = slice(16 * p, 16 * (p + 1))
        q = queries[heads, :]
        spread_q = jnp.concatenate([jnp.where(top, q, 0.0), jnp.where(top, 0.0, q)], axis=1)
        scores = lax.dot_general(
            spread_q.astype(BF16),
            keys[:, cols],
            (((1,), (1,)), ((), ())),
            preferred_element_type=F32,
        )
        scores = jnp.where(live, scores * kscale[heads, :], MASKED_SCORE)
        own_key = jnp.where(top, new_key[2 * p : 2 * p + 1], new_key[2 * p + 1 : 2 * p + 2])
        own_value = jnp.where(top, new_value[2 * p : 2 * p + 1], new_value[2 * p + 1 : 2 * p + 2])
        own_score = jnp.sum(q * own_key, axis=1, keepdims=True) * inv_root
        peak = jnp.maximum(jnp.max(scores, axis=1, keepdims=True), own_score)
        probs = jnp.exp(scores - peak)
        own_prob = jnp.exp(own_score - peak)
        total = jnp.sum(probs, axis=1, keepdims=True) + own_prob
        weighted = (probs * vscale[heads, :]).astype(BF16)
        mixed = jnp.dot(weighted, values[:, cols], preferred_element_type=F32)
        mixed = jnp.where(top, mixed[:, :LANES], mixed[:, LANES:])
        mixed = mixed + own_prob.astype(BF16).astype(F32) * own_value
        c_src[heads, :] = (mixed / total).astype(BF16).astype(F32)

    spread(2, c_src, c1, c2_src, c2)
    gather(2, c_src, c1, c2_src, c2)
    loads[7].wait()
    low, high = gathered(2, c2_src, c2)
    reduce_start(3, (matmul(low, high, wo),), d1_src, d1)
    rows_start(3, reduce_end(3, d1_src, d1), d2_src, d2)
    wait_recv(copy_y, ny, gy, 3, tile(d2_src), tile(d2))
    for j in range(per):
        rows[pl.ds(j, ny, stride=per), :] = d2[pl.ds(j, ny, stride=8), :]
    out_ref[...] = (wide[...] + rows[...]).astype(BF16)

    wait_send(copy_x, nx, gx, 0, tile(normed), tile(a1))
    wait_send(copy_y, ny, gy, 0, whole(a2_src), lead(a2))
    wait_send(copy_x, nx, gx, 1, lead(b1_src), lead(b1))
    wait_send(copy_y, ny, gy, 1, tile(b2_src), tile(b2))
    wait_send(copy_x, nx, gx, 2, tile(c_src), tile(c1))
    wait_send(copy_y, ny, gy, 2, whole(c2_src), lead(c2))
    wait_send(copy_x, nx, gx, 3, lead(d1_src), lead(d1))
    wait_send(copy_y, ny, gy, 3, tile(d2_src), tile(d2))


def body(
    nx,
    ny,
    hidden_in,
    norm_gain,
    w_query,
    key_weight,
    value_weight,
    w_output,
    key_cache_units,
    value_cache_units,
    key_scale,
    value_block_scale,
    lengths,
):
    width = hidden_in.shape[1]
    chunks = width // LANES
    depth, query_cols = w_query.shape
    key_cols = key_weight.shape[1]
    slots, cache_cols = key_cache_units.shape[1:]
    blocks = key_scale.shape[1]
    cols = query_cols + 2 * key_cols
    count = nx * ny
    any_space = pl.BlockSpec(memory_space=pl.ANY)
    smem = pl.BlockSpec(memory_space=pltpu.SMEM)
    vmem = pltpu.VMEM
    out = pl.pallas_call(
        functools.partial(kernel, nx, ny),
        out_shape=jax.ShapeDtypeStruct((chunks, LANES), BF16),
        in_specs=[any_space] * 8 + [smem] * 3,
        out_specs=pl.BlockSpec(memory_space=pltpu.VMEM),
        scratch_shapes=[
            vmem((1, width), BF16),
            vmem((chunks, LANES), F32),
            vmem((depth, query_cols), BF16),
            vmem((depth, key_cols), BF16),
            vmem((depth, key_cols), BF16),
            vmem((depth, 2 * key_cols), BF16),
            vmem((depth, query_cols), BF16),
            vmem((slots, cache_cols), BF16),
            vmem((slots, cache_cols), BF16),
            vmem((chunks, LANES), F32),
            vmem((chunks, LANES), F32),
            vmem((nx * 8, LANES), F32),
            vmem((16, depth // 2), BF16),
            vmem((ny, 16, depth // 2), BF16),
            vmem((cols // LANES, count, LANES), F32),
            vmem((nx, ny, cols), F32),
            vmem((nx, ny, cols), F32),
            vmem((ny * 8, LANES), F32),
            vmem((ny * 8, LANES), F32),
            vmem((chunks, LANES), F32),
            vmem((chunks, LANES), F32),
            vmem((chunks, slots), F32),
            vmem((chunks, slots), F32),
            vmem((chunks, LANES), F32),
            vmem((nx * 8, LANES), F32),
            vmem((16, depth // 2), BF16),
            vmem((ny, 16, depth // 2), BF16),
            vmem((nx, ny, query_cols), F32),
            vmem((nx, ny, query_cols), F32),
            vmem((ny * 8, LANES), F32),
            vmem((ny * 8, LANES), F32),
            pltpu.SemaphoreType.DMA((8,)),
            pltpu.SemaphoreType.DMA((4, nx)),
            pltpu.SemaphoreType.DMA((4, nx)),
            pltpu.SemaphoreType.DMA((4, ny)),
            pltpu.SemaphoreType.DMA((4, ny)),
        ],
        compiler_params=pltpu.CompilerParams(
            collective_id=0, has_side_effects=True, vmem_limit_bytes=48 * 1024 * 1024
        ),
    )(
        hidden_in,
        norm_gain.reshape(chunks, LANES),
        w_query,
        key_weight,
        value_weight,
        w_output,
        key_cache_units.reshape(slots, cache_cols),
        value_cache_units.reshape(slots, cache_cols),
        key_scale.reshape(blocks, GROUPS),
        value_block_scale.reshape(blocks, GROUPS),
        lengths,
    )
    return out.reshape(1, width)


def solution(mesh):
    placed = (
        P(("gx", "gy"), None),
        P(),
        P("gx", "gy"),
        P("gx", "gy"),
        P("gx", "gy"),
        P("gx", "gy"),
        P(("gx", "gy"), None, None),
        P(("gx", "gy"), None, None),
        P(("gx", "gy"), None, None),
        P(("gx", "gy"), None, None),
        P(("gx", "gy")),
    )
    return jax.shard_map(
        functools.partial(body, mesh.shape["gx"], mesh.shape["gy"]),
        mesh=mesh,
        in_specs=placed,
        out_specs=P(("gx", "gy"), None),
        check_vma=False,
    )
```

```python
import functools
import math

import jax
import jax.numpy as jnp
from jax import lax
from jax.experimental import pallas as pl
from jax.experimental.pallas import tpu as pltpu
from jax.sharding import PartitionSpec as P

MESH = pl.DeviceIdType.MESH
F32 = jnp.float32
BF16 = jnp.bfloat16

GROUPS = 8
LANES = 128
ROPE_BASE = 500000.0
NORM_EPS = 1e-05
MASKED_SCORE = -1e30


def kernel(
    nx,
    ny,
    hidden_hbm,
    gain_hbm,
    wq_hbm,
    wk_hbm,
    wv_hbm,
    wo_hbm,
    keys_hbm,
    values_hbm,
    key_scale,
    value_scale,
    lengths,
    out_ref,
    hidden,
    gain,
    wq,
    wkv,
    wo,
    keys,
    values,
    wide,
    normed,
    a1,
    a2_src,
    a2,
    prod,
    b1_src,
    b1,
    b2_src,
    b2,
    rows,
    queries,
    kscale,
    vscale,
    c_src,
    c1,
    c2_src,
    c2,
    d1_src,
    d1,
    d2_src,
    d2,
    load_sem,
    send_x,
    recv_x,
    send_y,
    recv_y,
):
    gx = lax.axis_index("gx")
    gy = lax.axis_index("gy")
    slots = keys.shape[0]
    blocks = slots // LANES

    key_cols = wk_hbm.shape[0]
    loads = [
        pltpu.make_async_copy(src, dst, load_sem.at[i])
        for i, (src, dst) in enumerate(
            (
                (hidden_hbm, hidden),
                (gain_hbm, gain),
                (wk_hbm, wkv.at[pl.ds(0, key_cols)]),
                (wv_hbm, wkv.at[pl.ds(key_cols, key_cols)]),
                (wq_hbm, wq),
                (keys_hbm, keys),
                (values_hbm, values),
                (wo_hbm, wo),
            )
        )
    ]
    for load in loads:
        load.start()

    barrier = pltpu.get_barrier_semaphore()

    @pl.loop(1, nx)
    def _(j):
        pl.semaphore_signal(
            barrier, inc=1, device_id=(lax.rem(gx + j, nx), gy), device_id_type=MESH
        )

    @pl.loop(1, ny)
    def _(j):
        pl.semaphore_signal(
            barrier, inc=1, device_id=(gx, lax.rem(gy + j, ny)), device_id_type=MESH
        )

    def copy_x(stage, src, dst, peer, slot):
        return pltpu.make_async_remote_copy(
            src_ref=src(peer),
            dst_ref=dst(slot),
            send_sem=send_x.at[stage, peer],
            recv_sem=recv_x.at[stage, slot],
            device_id=(peer, gy),
            device_id_type=MESH,
        )

    def copy_y(stage, src, dst, peer, slot):
        return pltpu.make_async_remote_copy(
            src_ref=src(peer),
            dst_ref=dst(slot),
            send_sem=send_y.at[stage, peer],
            recv_sem=recv_y.at[stage, slot],
            device_id=(gx, peer),
            device_id_type=MESH,
        )

    pending = []

    def start_all(copy, n, me, stage, src, dst):
        pending.append((copy, n, me, stage, src, dst))

        @pl.loop(1, n)
        def _(j):
            copy(stage, src, dst, lax.rem(me + j, n), me).start()

    def wait_recv(copy, n, me, stage, src, dst):
        @pl.loop(1, n)
        def _(j):
            peer = lax.rem(me + j, n)
            copy(stage, src, dst, peer, peer).wait_recv()

    def wait_send(copy, n, me, stage, src, dst):
        @pl.loop(1, n)
        def _(j):
            copy(stage, src, dst, lax.rem(me + j, n), me).wait_send()

    def tile(ref, count=8):
        return lambda i: ref.at[pl.ds(pl.multiple_of(i * count, count), count)]

    def lead(ref):
        return lambda i: ref.at[i]

    def whole(ref):
        return lambda i: ref

    loads[0].wait()
    row = hidden[...].astype(F32)
    for s in range(wide.shape[0]):
        wide[s : s + 1, :] = row[:, s * LANES : (s + 1) * LANES]
    loads[1].wait()
    x = wide[...]
    variance = jnp.sum(jnp.sum(x * x, axis=0, keepdims=True), axis=1, keepdims=True) * (
        1.0 / (x.shape[0] * LANES)
    )
    normed[...] = (x * lax.rsqrt(variance + NORM_EPS) * gain[...]).astype(BF16).astype(F32)

    pl.semaphore_wait(barrier, nx + ny - 2)

    def spread(stage, src, first, second_src, second):
        start_all(copy_x, nx, gx, stage, tile(src), tile(first))
        own = pl.multiple_of(gx * 8, 8)
        first[pl.ds(own, 8), :] = src[pl.ds(own, 8), :]

    def gather(stage, src, first, second_src, second):
        wait_recv(copy_x, nx, gx, stage, tile(src), tile(first))
        chunks = [first[pl.ds(s, nx, stride=8), :] for s in range(8)]
        halves = jnp.concatenate(
            [jnp.concatenate(chunks[:4], axis=1), jnp.concatenate(chunks[4:], axis=1)], axis=0
        ).astype(BF16)
        second_src[...] = halves
        start_all(copy_y, ny, gy, stage, whole(second_src), lead(second))
        second[gy] = halves

    def gathered(stage, second_src, second):
        wait_recv(copy_y, ny, gy, stage, whole(second_src), lead(second))
        both = second[...].astype(F32)
        count = nx * ny
        width = both.shape[-1]
        return (
            both[:, :8].reshape(count, width).astype(BF16),
            both[:, 8:].reshape(count, width).astype(BF16),
        )

    spread(0, normed, a1, a2_src, a2)

    length = lengths[0]
    lane = lax.broadcasted_iota(jnp.int32, (1, LANES), 1)
    step = (lane % 64).astype(F32)
    angle = length.astype(F32) * jnp.exp(step * (-2.0 * math.log(ROPE_BASE) / LANES))
    cosine = jnp.cos(angle)
    sine = jnp.sin(angle)
    sine = jnp.where(lane < 64, -sine, sine)
    inv_root = 1.0 / math.sqrt(LANES)

    gather(0, normed, a1, a2_src, a2)

    @pl.loop(0, blocks)
    def _(b):
        at = pl.ds(pl.multiple_of(b * LANES, LANES), LANES)
        for g in range(GROUPS):
            kscale[8 * g : 8 * g + 8, at] = jnp.full((8, LANES), key_scale[g, b] * inv_root, F32)
            vscale[8 * g : 8 * g + 8, at] = jnp.full((8, LANES), value_scale[g, b], F32)

    loads[2].wait()
    loads[3].wait()
    loads[4].wait()

    half = wq.shape[0] // 2

    def matmul(low, high, weights):
        return jnp.dot(low, weights[:half], preferred_element_type=F32) + jnp.dot(
            high, weights[half:], preferred_element_type=F32
        )

    def matmul_nt(low, high, weights):
        dims = (((1,), (1,)), ((), ()))
        return lax.dot_general(
            low, weights[:, :half], dims, preferred_element_type=F32
        ) + lax.dot_general(high, weights[:, half:], dims, preferred_element_type=F32)

    def reduce_start(stage, parts, src, dst):
        at = 0
        for part in parts:
            for c in range(part.shape[1] // LANES):
                prod[at] = part[:, c * LANES : (c + 1) * LANES]
                at += 1
        for target in range(nx):
            for c in range(at):
                src[target, :, c * LANES : (c + 1) * LANES] = prod.at[c][
                    pl.ds(target, ny, stride=nx), :
                ]
        start_all(copy_x, nx, gx, stage, lead(src), lead(dst))
        dst[gx] = src[gx]

    def reduce_end(stage, src, dst):
        wait_recv(copy_x, nx, gx, stage, lead(src), lead(dst))
        total = dst[0]
        for i in range(1, nx):
            total = total + dst[i]
        return total

    def rows_start(stage, summed, src, dst):
        for c in range(summed.shape[1] // LANES):
            src[pl.ds(c, ny, stride=8), :] = summed[:, c * LANES : (c + 1) * LANES]
        start_all(copy_y, ny, gy, stage, tile(src), tile(dst))
        own = pl.multiple_of(gy * 8, 8)
        dst[pl.ds(own, 8), :] = src[pl.ds(own, 8), :]

    low, high = gathered(0, a2_src, a2)
    reduce_start(1, (matmul(low, high, wq), matmul_nt(low, high, wkv)), b1_src, b1)
    b2_src[...] = jnp.zeros_like(b2_src)
    d2_src[...] = jnp.zeros_like(d2_src)
    summed = reduce_end(1, b1_src, b1).astype(BF16).astype(F32)
    rows_start(1, summed, b2_src, b2)
    wait_recv(copy_y, ny, gy, 1, tile(b2_src), tile(b2))

    per = wq.shape[1] // LANES
    for j in range(per):
        rows[pl.ds(j, ny, stride=per), :] = b2[pl.ds(j, ny, stride=8), :]
    even = b2[pl.ds(per, ny // 2, stride=16), :]
    odd = b2[pl.ds(per + 8, ny // 2, stride=16), :]
    front = lane < 64
    new_key = jnp.where(front, even, pltpu.roll(odd, 64, 1))
    new_value = jnp.where(front, pltpu.roll(even, 64, 1), odd)

    def rotate(v):
        return (v * cosine + pltpu.roll(v, 64, 1) * sine).astype(BF16).astype(F32)

    new_key = rotate(new_key)
    queries[...] = rotate(rows[...])

    loads[5].wait()
    loads[6].wait()
    top = lax.broadcasted_iota(jnp.int32, (16, LANES), 0) < 8
    live = lax.broadcasted_iota(jnp.int32, (1, slots), 1) < length
    for p in range(GROUPS // 2):
        cols = slice(2 * p * LANES, 2 * (p + 1) * LANES)
        heads = slice(16 * p, 16 * (p + 1))
        q = queries[heads, :]
        spread_q = jnp.concatenate([jnp.where(top, q, 0.0), jnp.where(top, 0.0, q)], axis=1)
        scores = lax.dot_general(
            spread_q.astype(BF16),
            keys[:, cols],
            (((1,), (1,)), ((), ())),
            preferred_element_type=F32,
        )
        scores = jnp.where(live, scores * kscale[heads, :], MASKED_SCORE)
        own_key = jnp.where(top, new_key[2 * p : 2 * p + 1], new_key[2 * p + 1 : 2 * p + 2])
        own_value = jnp.where(top, new_value[2 * p : 2 * p + 1], new_value[2 * p + 1 : 2 * p + 2])
        own_score = jnp.sum(q * own_key, axis=1, keepdims=True) * inv_root
        peak = jnp.maximum(jnp.max(scores, axis=1, keepdims=True), own_score)
        probs = jnp.exp(scores - peak)
        own_prob = jnp.exp(own_score - peak)
        total = jnp.sum(probs, axis=1, keepdims=True) + own_prob
        weighted = (probs * vscale[heads, :]).astype(BF16)
        mixed = jnp.dot(weighted, values[:, cols], preferred_element_type=F32)
        mixed = jnp.where(top, mixed[:, :LANES], mixed[:, LANES:])
        mixed = mixed + own_prob.astype(BF16).astype(F32) * own_value
        c_src[heads, :] = (mixed / total).astype(BF16).astype(F32)

    spread(2, c_src, c1, c2_src, c2)
    gather(2, c_src, c1, c2_src, c2)
    loads[7].wait()
    low, high = gathered(2, c2_src, c2)
    reduce_start(3, (matmul(low, high, wo),), d1_src, d1)
    rows_start(3, reduce_end(3, d1_src, d1), d2_src, d2)
    wait_recv(copy_y, ny, gy, 3, tile(d2_src), tile(d2))
    for j in range(per):
        rows[pl.ds(j, ny, stride=per), :] = d2[pl.ds(j, ny, stride=8), :]
    out_ref[...] = (wide[...] + rows[...]).astype(BF16)

    for sent in pending:
        wait_send(*sent)


def body(
    nx,
    ny,
    hidden_in,
    norm_gain,
    w_query,
    key_weight,
    value_weight,
    w_output,
    key_cache_units,
    value_cache_units,
    key_scale,
    value_block_scale,
    lengths,
):
    width = hidden_in.shape[1]
    chunks = width // LANES
    depth, query_cols = w_query.shape
    key_cols = key_weight.shape[1]
    slots, cache_cols = key_cache_units.shape[1:]
    blocks = key_scale.shape[1]
    cols = query_cols + 2 * key_cols
    count = nx * ny
    any_space = pl.BlockSpec(memory_space=pl.ANY)
    smem = pl.BlockSpec(memory_space=pltpu.SMEM)
    vmem = pltpu.VMEM
    out = pl.pallas_call(
        functools.partial(kernel, nx, ny),
        out_shape=jax.ShapeDtypeStruct((chunks, LANES), BF16),
        in_specs=[any_space] * 8 + [smem] * 3,
        out_specs=pl.BlockSpec(memory_space=pltpu.VMEM),
        scratch_shapes=[
            vmem((1, width), BF16),
            vmem((chunks, LANES), F32),
            vmem((depth, query_cols), BF16),
            vmem((2 * key_cols, depth), BF16),
            vmem((depth, query_cols), BF16),
            vmem((slots, cache_cols), BF16),
            vmem((slots, cache_cols), BF16),
            vmem((chunks, LANES), F32),
            vmem((chunks, LANES), F32),
            vmem((nx * 8, LANES), F32),
            vmem((16, depth // 2), BF16),
            vmem((ny, 16, depth // 2), BF16),
            vmem((cols // LANES, count, LANES), F32),
            vmem((nx, ny, cols), F32),
            vmem((nx, ny, cols), F32),
            vmem((ny * 8, LANES), F32),
            vmem((ny * 8, LANES), F32),
            vmem((chunks, LANES), F32),
            vmem((chunks, LANES), F32),
            vmem((chunks, slots), F32),
            vmem((chunks, slots), F32),
            vmem((chunks, LANES), F32),
            vmem((nx * 8, LANES), F32),
            vmem((16, depth // 2), BF16),
            vmem((ny, 16, depth // 2), BF16),
            vmem((nx, ny, query_cols), F32),
            vmem((nx, ny, query_cols), F32),
            vmem((ny * 8, LANES), F32),
            vmem((ny * 8, LANES), F32),
            pltpu.SemaphoreType.DMA((8,)),
            pltpu.SemaphoreType.DMA((4, nx)),
            pltpu.SemaphoreType.DMA((4, nx)),
            pltpu.SemaphoreType.DMA((4, ny)),
            pltpu.SemaphoreType.DMA((4, ny)),
        ],
        compiler_params=pltpu.CompilerParams(
            collective_id=0, has_side_effects=True, vmem_limit_bytes=63 * 1024 * 1024
        ),
    )(
        hidden_in,
        norm_gain.reshape(chunks, LANES),
        w_query,
        key_weight.T,
        value_weight.T,
        w_output,
        key_cache_units.reshape(slots, cache_cols),
        value_cache_units.reshape(slots, cache_cols),
        key_scale.reshape(blocks, GROUPS).T,
        value_block_scale.reshape(blocks, GROUPS).T,
        lengths,
    )
    return out.reshape(1, width)


def solution(mesh):
    placed = (
        P(("gx", "gy"), None),
        P(),
        P("gx", "gy"),
        P("gx", "gy"),
        P("gx", "gy"),
        P("gx", "gy"),
        P(("gx", "gy"), None, None),
        P(("gx", "gy"), None, None),
        P(("gx", "gy"), None, None),
        P(("gx", "gy"), None, None),
        P(("gx", "gy")),
    )
    return jax.shard_map(
        functools.partial(body, mesh.shape["gx"], mesh.shape["gy"]),
        mesh=mesh,
        in_specs=placed,
        out_specs=P(("gx", "gy"), None),
        check_vma=False,
    )
```

```python
import functools
import math

import jax
import jax.numpy as jnp
from jax import lax
from jax.experimental import pallas as pl
from jax.experimental.pallas import tpu as pltpu
from jax.sharding import PartitionSpec as P

MESH = pl.DeviceIdType.MESH
F32 = jnp.float32
BF16 = jnp.bfloat16

GROUPS = 8
LANES = 128
ROPE_BASE = 500000.0
NORM_EPS = 1e-05
MASKED_SCORE = -1e30


def kernel(
    nz,
    ny,
    hidden_hbm,
    gain_hbm,
    wq_hbm,
    wk_hbm,
    wv_hbm,
    wo_hbm,
    keys_hbm,
    values_hbm,
    key_scale,
    value_scale,
    lengths,
    out_ref,
    hidden,
    gain,
    wq,
    wkv,
    wo,
    keys,
    values,
    wide,
    normed,
    a_both,
    a_src,
    a_dst,
    spare,
    b_give,
    b_take,
    b_src,
    b_dst,
    heads_in,
    rows,
    queries,
    kscale,
    vscale,
    mixed_out,
    c_both,
    c_src,
    c_dst,
    d_give,
    d_take,
    d_src,
    d_dst,
    load_sem,
    send_core,
    recv_core,
    send_far,
    recv_far,
):
    gx = lax.axis_index("gx")
    gy = lax.axis_index("gy")
    z, core = gx // 2, lax.rem(gx, 2)
    other = 1 - core
    side = 4
    px, py = gy // side, lax.rem(gy, side)
    chips = nz * ny
    chip = z * ny + gy
    slots = keys.shape[0]
    blocks = slots // LANES

    key_cols = wk_hbm.shape[0]
    loads = [
        pltpu.make_async_copy(src, dst, load_sem.at[i])
        for i, (src, dst) in enumerate(
            (
                (hidden_hbm, hidden),
                (gain_hbm, gain),
                (wk_hbm, wkv.at[pl.ds(0, key_cols)]),
                (wv_hbm, wkv.at[pl.ds(key_cols, key_cols)]),
                (wq_hbm, wq),
                (keys_hbm, keys),
                (values_hbm, values),
                (wo_hbm, wo),
            )
        )
    ]
    for load in loads:
        load.start()

    def away(i):
        return jnp.where(i == 3, 0, jnp.where(i == 2, 3, 2 - i))

    def plane(i):
        return lax.rem(px + away(i // side), side) * side + lax.rem(
            py + away(lax.rem(i, side)), side
        )

    def layer(i):
        return lax.rem(z + away(i), nz)

    barrier = pltpu.get_barrier_semaphore()

    @pl.loop(0, chips - 1)
    def _(i):
        target = (layer(i // ny) * 2 + core, plane(lax.rem(i, ny)))
        pl.semaphore_signal(barrier, inc=1, device_id=target, device_id_type=MESH)

    pl.semaphore_signal(barrier, inc=1, device_id=(z * 2 + other, gy), device_id_type=MESH)

    def to_core(i, src, dst):
        return pltpu.make_async_remote_copy(
            src_ref=src,
            dst_ref=dst,
            send_sem=send_core.at[i],
            recv_sem=recv_core.at[i],
            device_id=(z * 2 + other, gy),
            device_id_type=MESH,
        )

    def to_chip(i, src, dst, tz, ty):
        return pltpu.make_async_remote_copy(
            src_ref=src,
            dst_ref=dst.at[chip],
            send_sem=send_far.at[i],
            recv_sem=recv_far.at[i],
            device_id=(tz * 2 + core, ty),
            device_id_type=MESH,
        )

    def to_all(i, src, dst):
        @pl.loop(0, chips - 1)
        def _(k):
            tz, ty = layer(k // ny), plane(lax.rem(k, ny))
            to_chip(i, src(tz, ty), dst, tz, ty).start()

    def wait_all(sem, ref):
        most = ref.at[pl.ds(0, chips - 1)]
        pltpu.make_async_copy(most, most, sem).wait()

    loads[0].wait()
    row = hidden[...].astype(F32)
    for s in range(wide.shape[0]):
        wide[s : s + 1, :] = row[:, s * LANES : (s + 1) * LANES]
    loads[1].wait()
    x = wide[...]
    variance = jnp.sum(jnp.sum(x * x, axis=0, keepdims=True), axis=1, keepdims=True) * (
        1.0 / (x.shape[0] * LANES)
    )
    x = (x * lax.rsqrt(variance + NORM_EPS) * gain[...]).astype(BF16).astype(F32)
    normed[...] = x.reshape(normed.shape)

    pl.semaphore_wait(barrier, chips)

    first = to_core(0, normed.at[:, other], a_both.at[:, core])
    first.start()
    for t in range(nz):
        a_both[t, core] = normed[t, core]

    length = lengths[0]
    lane = lax.broadcasted_iota(jnp.int32, (1, LANES), 1)
    step = (lane % 64).astype(F32)
    angle = length.astype(F32) * jnp.exp(step * (-2.0 * math.log(ROPE_BASE) / LANES))
    inv_root = 1.0 / math.sqrt(LANES)

    first.wait_recv()
    a_src[...] = a_both[...].reshape(a_src.shape).astype(BF16)
    to_all(0, lambda tz, ty: a_src.at[tz], a_dst)
    a_dst[chip] = a_src[z]

    cosine = jnp.cos(angle)
    sine = jnp.sin(angle)
    sine = jnp.where(lane < 64, -sine, sine)

    @pl.loop(0, blocks)
    def _(b):
        at = pl.ds(pl.multiple_of(b * LANES, LANES), LANES)
        for g in range(GROUPS):
            kscale[8 * g : 8 * g + 8, at] = jnp.full((8, LANES), key_scale[g, b] * inv_root, F32)
            vscale[8 * g : 8 * g + 8, at] = jnp.full((8, LANES), value_scale[g, b], F32)

    loads[2].wait()
    loads[3].wait()
    loads[4].wait()

    def requests(r):
        chunks = [spare[pl.ds(r * 8 + s, chips, stride=16), :] for s in range(8)]
        return jnp.concatenate(chunks, axis=1).astype(BF16)

    nt = (((1,), (1,)), ((), ()))

    def project(r):
        lhs = requests(r)
        return jnp.concatenate(
            [
                jnp.dot(lhs, wq[...], preferred_element_type=F32),
                lax.dot_general(lhs, wkv[...], nt, preferred_element_type=F32),
            ],
            axis=1,
        )

    def project_out(r):
        return jnp.dot(requests(r), wo[...], preferred_element_type=F32)

    def reduce(i, product, arrived, give, take, src, dst):
        spare[...] = arrived[...].astype(F32).reshape(spare.shape)
        give[...] = product(other)
        swap = to_core(i, give, take)
        swap.start()
        kept = product(core)
        swap.wait_recv()
        total = kept + take[...]
        for c in range(total.shape[1] // LANES):
            src[:, c, :] = total[:, c * LANES : (c + 1) * LANES]
        to_all(i, lambda tz, ty: src.at[tz * ny + ty], dst)
        dst[chip] = src[chip]
        wait_all(recv_far.at[i], dst)
        summed = dst[0:ny]
        for t in range(1, nz):
            summed = summed + dst[t * ny : (t + 1) * ny]
        return swap, summed

    wait_all(recv_far.at[0], a_dst)
    second, summed = reduce(1, project, a_dst, b_give, b_take, b_src, b_dst)
    heads_in[:, 0 : summed.shape[1], :] = summed.astype(BF16).astype(F32)

    per = wq.shape[1] // LANES
    for j in range(per):
        rows[pl.ds(j, ny, stride=per), :] = heads_in[:, j, :]
    both = heads_in[:, per, :]
    queries[0:ny, :] = both
    even = queries[pl.ds(0, ny // 2, stride=2), :]
    odd = queries[pl.ds(1, ny // 2, stride=2), :]
    front = lane < 64
    new_key = jnp.where(front, even, pltpu.roll(odd, 64, 1))
    new_value = jnp.where(front, pltpu.roll(even, 64, 1), odd)

    def rotate(v):
        return (v * cosine + pltpu.roll(v, 64, 1) * sine).astype(BF16).astype(F32)

    heads_in[0, :, :] = rotate(new_key)
    heads_in[1, :, :] = new_value
    queries[...] = rotate(rows[...])

    loads[5].wait()
    loads[6].wait()
    top = lax.broadcasted_iota(jnp.int32, (16, LANES), 0) < 8
    live = lax.broadcasted_iota(jnp.int32, (1, slots), 1) < length

    def attend(p):
        cols = pl.ds(pl.multiple_of(2 * p * LANES, 2 * LANES), 2 * LANES)
        heads = pl.ds(pl.multiple_of(16 * p, 16), 16)
        q = queries[heads, :]
        spread_q = jnp.concatenate([jnp.where(top, q, 0.0), jnp.where(top, 0.0, q)], axis=1)
        scores = lax.dot_general(
            spread_q.astype(BF16), keys[:, cols], nt, preferred_element_type=F32
        )
        scores = jnp.where(live, scores * kscale[heads, :], MASKED_SCORE)
        own_key = jnp.where(
            top, heads_in[0, pl.ds(2 * p, 1), :], heads_in[0, pl.ds(2 * p + 1, 1), :]
        )
        own_value = jnp.where(
            top, heads_in[1, pl.ds(2 * p, 1), :], heads_in[1, pl.ds(2 * p + 1, 1), :]
        )
        own_score = jnp.sum(q * own_key, axis=1, keepdims=True) * inv_root
        peak = jnp.maximum(jnp.max(scores, axis=1, keepdims=True), own_score)
        probs = jnp.exp(scores - peak)
        own_prob = jnp.exp(own_score - peak)
        total = jnp.sum(probs, axis=1, keepdims=True) + own_prob
        weighted = (probs * vscale[heads, :]).astype(BF16)
        mixed = jnp.dot(weighted, values[:, cols], preferred_element_type=F32)
        mixed = jnp.where(top, mixed[:, :LANES], mixed[:, LANES:])
        mixed = mixed + own_prob.astype(BF16).astype(F32) * own_value
        mixed = (mixed / total).astype(BF16).astype(F32)
        mixed_out[p] = mixed.reshape(2, 8, LANES)

    def pair(k):
        p = layer(k)
        return to_core(2 + k, mixed_out.at[p, other], c_both.at[p, core])

    def finish(k):
        p = layer(k)
        c_both[p, core] = mixed_out[p, core]
        pair(k).wait_recv()
        c_src[p] = c_both[p].reshape(16, LANES).astype(BF16)

        @pl.loop(0, ny if k < nz - 1 else ny - 1)
        def _(i):
            to_chip(2, c_src.at[p], c_dst, p, plane(i)).start()

    for k in range(nz):
        attend(layer(k))
        pair(k).start()
        if k > 0:
            finish(k - 1)
    finish(nz - 1)
    c_dst[chip] = c_src[z]

    loads[7].wait()
    wait_all(recv_far.at[2], c_dst)
    third, summed = reduce(6, project_out, c_dst, d_give, d_take, d_src, d_dst)
    for j in range(per):
        rows[pl.ds(j, ny, stride=per), :] = summed[:, j, :]
    out_ref[...] = (wide[...] + rows[...]).astype(BF16)

    first.wait_send()
    second.wait_send()
    third.wait_send()
    for k in range(nz):
        pair(k).wait_send()
    wait_all(send_far.at[0], a_dst)
    wait_all(send_far.at[1], b_dst)
    wait_all(send_far.at[2], c_dst)
    wait_all(send_far.at[6], d_dst)


def body(
    nx,
    ny,
    hidden_in,
    norm_gain,
    w_query,
    key_weight,
    value_weight,
    w_output,
    key_cache_units,
    value_cache_units,
    key_scale,
    value_block_scale,
    lengths,
):
    width = hidden_in.shape[1]
    chunks = width // LANES
    depth, query_cols = w_query.shape
    key_cols = key_weight.shape[1]
    slots, cache_cols = key_cache_units.shape[1:]
    blocks = key_scale.shape[1]
    cols = query_cols + 2 * key_cols
    nz = nx // 2
    chips = nz * ny
    any_space = pl.BlockSpec(memory_space=pl.ANY)
    smem = pl.BlockSpec(memory_space=pltpu.SMEM)
    vmem = pltpu.VMEM
    out = pl.pallas_call(
        functools.partial(kernel, nz, ny),
        out_shape=jax.ShapeDtypeStruct((chunks, LANES), BF16),
        in_specs=[any_space] * 8 + [smem] * 3,
        out_specs=pl.BlockSpec(memory_space=pltpu.VMEM),
        scratch_shapes=[
            vmem((1, width), BF16),
            vmem((chunks, LANES), F32),
            vmem((depth, query_cols), BF16),
            vmem((2 * key_cols, depth), BF16),
            vmem((depth, query_cols), BF16),
            vmem((slots, cache_cols), BF16),
            vmem((slots, cache_cols), BF16),
            vmem((chunks, LANES), F32),
            vmem((nz, 2, 8, LANES), F32),
            vmem((nz, 2, 8, LANES), F32),
            vmem((nz, 16, LANES), BF16),
            vmem((chips, 16, LANES), BF16),
            vmem((chips * 16, LANES), F32),
            vmem((chips, cols), F32),
            vmem((chips, cols), F32),
            vmem((chips, cols // LANES, LANES), F32),
            vmem((chips, cols // LANES, LANES), F32),
            vmem((ny, 8, LANES), F32),
            vmem((chunks, LANES), F32),
            vmem((chunks, LANES), F32),
            vmem((chunks, slots), F32),
            vmem((chunks, slots), F32),
            vmem((nz, 2, 8, LANES), F32),
            vmem((nz, 2, 8, LANES), F32),
            vmem((nz, 16, LANES), BF16),
            vmem((chips, 16, LANES), BF16),
            vmem((chips, query_cols), F32),
            vmem((chips, query_cols), F32),
            vmem((chips, query_cols // LANES, LANES), F32),
            vmem((chips, query_cols // LANES, LANES), F32),
            pltpu.SemaphoreType.DMA((8,)),
            pltpu.SemaphoreType.DMA((7,)),
            pltpu.SemaphoreType.DMA((7,)),
            pltpu.SemaphoreType.DMA((7,)),
            pltpu.SemaphoreType.DMA((7,)),
        ],
        compiler_params=pltpu.CompilerParams(
            collective_id=0, has_side_effects=True, vmem_limit_bytes=63 * 1024 * 1024
        ),
    )(
        hidden_in,
        norm_gain.reshape(chunks, LANES),
        w_query,
        key_weight.T,
        value_weight.T,
        w_output,
        key_cache_units.reshape(slots, cache_cols),
        value_cache_units.reshape(slots, cache_cols),
        key_scale.reshape(blocks, GROUPS).T,
        value_block_scale.reshape(blocks, GROUPS).T,
        lengths,
    )
    return out.reshape(1, width)


def solution(mesh):
    placed = (
        P(("gx", "gy"), None),
        P(),
        P("gx", "gy"),
        P("gx", "gy"),
        P("gx", "gy"),
        P("gx", "gy"),
        P(("gx", "gy"), None, None),
        P(("gx", "gy"), None, None),
        P(("gx", "gy"), None, None),
        P(("gx", "gy"), None, None),
        P(("gx", "gy")),
    )
    return jax.shard_map(
        functools.partial(body, mesh.shape["gx"], mesh.shape["gy"]),
        mesh=mesh,
        in_specs=placed,
        out_specs=P(("gx", "gy"), None),
        check_vma=False,
    )
```

```python
import functools
import math

import jax
import jax.numpy as jnp
from jax import lax
from jax.experimental import pallas as pl
from jax.experimental.pallas import tpu as pltpu
from jax.sharding import PartitionSpec as P

MESH = pl.DeviceIdType.MESH
F32 = jnp.float32
BF16 = jnp.bfloat16

GROUPS = 8
LANES = 128
ROPE_BASE = 500000.0
NORM_EPS = 1e-05
MASKED_SCORE = -1e30


def kernel(
    nz,
    ny,
    hidden_hbm,
    gain_hbm,
    wq_hbm,
    wk_hbm,
    wv_hbm,
    wo_hbm,
    keys_hbm,
    values_hbm,
    key_scale,
    value_scale,
    lengths,
    out_ref,
    hidden,
    gain,
    wq,
    wkv,
    wo,
    keys,
    values,
    wide,
    normed,
    a_both,
    a_src,
    a_dst,
    spare,
    b_give,
    b_take,
    b_src,
    b_dst,
    heads_in,
    rows,
    queries,
    kscale,
    vscale,
    mixed_out,
    c_both,
    c_src,
    c_dst,
    d_give,
    d_take,
    d_src,
    d_dst,
    load_sem,
    send_core,
    recv_core,
    send_far,
    recv_far,
    plane_in,
):
    gx = lax.axis_index("gx")
    gy = lax.axis_index("gy")
    z, core = gx // 2, lax.rem(gx, 2)
    other = 1 - core
    side = 4
    px, py = gy // side, lax.rem(gy, side)
    chips = nz * ny
    chip = z * ny + gy
    slots = keys.shape[0]
    blocks = slots // LANES

    key_cols = wk_hbm.shape[0]
    loads = [
        pltpu.make_async_copy(src, dst, load_sem.at[i])
        for i, (src, dst) in enumerate(
            (
                (hidden_hbm, hidden),
                (gain_hbm, gain),
                (wk_hbm, wkv.at[pl.ds(0, key_cols)]),
                (wv_hbm, wkv.at[pl.ds(key_cols, key_cols)]),
                (wq_hbm, wq),
                (keys_hbm, keys),
                (values_hbm, values),
                (wo_hbm, wo),
            )
        )
    ]
    loads[0].start()
    loads[1].start()

    def away(i):
        return jnp.where(i == 3, 0, jnp.where(i == 2, 3, 2 - i))

    def plane(i):
        return lax.rem(px + away(i // side), side) * side + lax.rem(
            py + away(lax.rem(i, side)), side
        )

    def layer(i):
        return lax.rem(z + away(i), nz)

    barrier = pltpu.get_barrier_semaphore()

    @pl.loop(0, ny - 1)
    def _(i):
        pl.semaphore_signal(barrier, inc=1, device_id=(gx, plane(i)), device_id_type=MESH)

    for i in range(nz - 1):
        pl.semaphore_signal(
            barrier, inc=1, device_id=(layer(i) * 2 + core, gy), device_id_type=MESH
        )
    pl.semaphore_signal(barrier, inc=1, device_id=(z * 2 + other, gy), device_id_type=MESH)

    for load in loads[2:]:
        load.start()

    def to_core(i, src, dst):
        return pltpu.make_async_remote_copy(
            src_ref=src,
            dst_ref=dst,
            send_sem=send_core.at[i],
            recv_sem=recv_core.at[i],
            device_id=(z * 2 + other, gy),
            device_id_type=MESH,
        )

    def to_chip(i, src, dst, tz, ty):
        return pltpu.make_async_remote_copy(
            src_ref=src,
            dst_ref=dst.at[chip],
            send_sem=send_far.at[i],
            recv_sem=recv_far.at[i],
            device_id=(tz * 2 + core, ty),
            device_id_type=MESH,
        )

    def to_all(i, src, dst):
        @pl.loop(0, chips - 1)
        def _(k):
            tz, ty = layer(k // ny), plane(lax.rem(k, ny))
            to_chip(i, src(tz, ty), dst, tz, ty).start()

    def wait_all(sem, ref):
        most = ref.at[pl.ds(0, chips - 1)]
        pltpu.make_async_copy(most, most, sem).wait()

    loads[0].wait()
    row = hidden[...].astype(F32)
    for s in range(wide.shape[0]):
        wide[s : s + 1, :] = row[:, s * LANES : (s + 1) * LANES]
    loads[1].wait()
    x = wide[...]
    variance = jnp.sum(jnp.sum(x * x, axis=0, keepdims=True), axis=1, keepdims=True) * (
        1.0 / (x.shape[0] * LANES)
    )
    x = (x * lax.rsqrt(variance + NORM_EPS) * gain[...]).astype(BF16).astype(F32)
    normed[...] = x.reshape(normed.shape)

    pl.semaphore_wait(barrier, ny + nz - 1)
    for i in range(nz - 1):
        pl.semaphore_signal(
            plane_in, inc=1, device_id=(layer(i) * 2 + core, gy), device_id_type=MESH
        )

    first = to_core(0, normed.at[:, other], a_both.at[:, core])
    first.start()
    for t in range(nz):
        a_both[t, core] = normed[t, core]

    length = lengths[0]
    lane = lax.broadcasted_iota(jnp.int32, (1, LANES), 1)
    step = (lane % 64).astype(F32)
    angle = length.astype(F32) * jnp.exp(step * (-2.0 * math.log(ROPE_BASE) / LANES))
    inv_root = 1.0 / math.sqrt(LANES)

    first.wait_recv()
    a_src[...] = a_both[...].reshape(a_src.shape).astype(BF16)

    @pl.loop(0, ny - 1)
    def _(i):
        to_chip(0, a_src.at[z], a_dst, z, plane(i)).start()

    pl.semaphore_wait(plane_in, nz - 1)

    @pl.loop(0, (nz - 1) * ny)
    def _(k):
        tz = layer(k // ny)
        to_chip(0, a_src.at[tz], a_dst, tz, plane(lax.rem(k, ny))).start()

    a_dst[chip] = a_src[z]

    cosine = jnp.cos(angle)
    sine = jnp.sin(angle)
    sine = jnp.where(lane < 64, -sine, sine)

    @pl.loop(0, blocks)
    def _(b):
        at = pl.ds(pl.multiple_of(b * LANES, LANES), LANES)
        for g in range(GROUPS):
            kscale[8 * g : 8 * g + 8, at] = jnp.full((8, LANES), key_scale[g, b] * inv_root, F32)
            vscale[8 * g : 8 * g + 8, at] = jnp.full((8, LANES), value_scale[g, b], F32)

    loads[2].wait()
    loads[3].wait()
    loads[4].wait()

    def requests(r):
        chunks = [spare[pl.ds(r * 8 + s, chips, stride=16), :] for s in range(8)]
        return jnp.concatenate(chunks, axis=1).astype(BF16)

    nt = (((1,), (1,)), ((), ()))

    def project(r):
        lhs = requests(r)
        return jnp.concatenate(
            [
                jnp.dot(lhs, wq[...], preferred_element_type=F32),
                lax.dot_general(lhs, wkv[...], nt, preferred_element_type=F32),
            ],
            axis=1,
        )

    def project_out(r):
        return jnp.dot(requests(r), wo[...], preferred_element_type=F32)

    def reduce(i, product, arrived, give, take, src, dst):
        spare[...] = arrived[...].astype(F32).reshape(spare.shape)
        give[...] = product(other)
        swap = to_core(i, give, take)
        swap.start()
        kept = product(core)
        swap.wait_recv()
        total = kept + take[...]
        for c in range(total.shape[1] // LANES):
            src[:, c, :] = total[:, c * LANES : (c + 1) * LANES]
        to_all(i, lambda tz, ty: src.at[tz * ny + ty], dst)
        dst[chip] = src[chip]
        wait_all(recv_far.at[i], dst)
        summed = dst[0:ny]
        for t in range(1, nz):
            summed = summed + dst[t * ny : (t + 1) * ny]
        return swap, summed

    wait_all(recv_far.at[0], a_dst)
    second, summed = reduce(1, project, a_dst, b_give, b_take, b_src, b_dst)
    heads_in[:, 0 : summed.shape[1], :] = summed.astype(BF16).astype(F32)

    per = wq.shape[1] // LANES
    for j in range(per):
        rows[pl.ds(j, ny, stride=per), :] = heads_in[:, j, :]
    both = heads_in[:, per, :]
    queries[0:ny, :] = both
    even = queries[pl.ds(0, ny // 2, stride=2), :]
    odd = queries[pl.ds(1, ny // 2, stride=2), :]
    front = lane < 64
    new_key = jnp.where(front, even, pltpu.roll(odd, 64, 1))
    new_value = jnp.where(front, pltpu.roll(even, 64, 1), odd)

    def rotate(v):
        return (v * cosine + pltpu.roll(v, 64, 1) * sine).astype(BF16).astype(F32)

    heads_in[0, :, :] = rotate(new_key)
    heads_in[1, :, :] = new_value
    queries[...] = rotate(rows[...])

    loads[5].wait()
    loads[6].wait()
    top = lax.broadcasted_iota(jnp.int32, (16, LANES), 0) < 8
    live = lax.broadcasted_iota(jnp.int32, (1, slots), 1) < length

    def score(p):
        cols = pl.ds(pl.multiple_of(2 * p * LANES, 2 * LANES), 2 * LANES)
        heads = pl.ds(pl.multiple_of(16 * p, 16), 16)
        q = queries[heads, :]
        spread_q = jnp.concatenate([jnp.where(top, q, 0.0), jnp.where(top, 0.0, q)], axis=1)
        scores = lax.dot_general(
            spread_q.astype(BF16), keys[:, cols], nt, preferred_element_type=F32
        )
        return jnp.where(live, scores * kscale[heads, :], MASKED_SCORE)

    def attend(p, scores):
        cols = pl.ds(pl.multiple_of(2 * p * LANES, 2 * LANES), 2 * LANES)
        heads = pl.ds(pl.multiple_of(16 * p, 16), 16)
        q = queries[heads, :]
        own_key = jnp.where(
            top, heads_in[0, pl.ds(2 * p, 1), :], heads_in[0, pl.ds(2 * p + 1, 1), :]
        )
        own_value = jnp.where(
            top, heads_in[1, pl.ds(2 * p, 1), :], heads_in[1, pl.ds(2 * p + 1, 1), :]
        )
        own_score = jnp.sum(q * own_key, axis=1, keepdims=True) * inv_root
        peak = jnp.maximum(jnp.max(scores, axis=1, keepdims=True), own_score)
        probs = jnp.exp(scores - peak)
        own_prob = jnp.exp(own_score - peak)
        total = jnp.sum(probs, axis=1, keepdims=True) + own_prob
        weighted = (probs * vscale[heads, :]).astype(BF16)
        mixed = jnp.dot(weighted, values[:, cols], preferred_element_type=F32)
        mixed = jnp.where(top, mixed[:, :LANES], mixed[:, LANES:])
        mixed = mixed + own_prob.astype(BF16).astype(F32) * own_value
        mixed = (mixed / total).astype(BF16).astype(F32)
        mixed_out[p] = mixed.reshape(2, 8, LANES)

    def pair(k):
        p = layer(k)
        return to_core(2 + k, mixed_out.at[p, other], c_both.at[p, core])

    def finish(k):
        p = layer(k)
        c_both[p, core] = mixed_out[p, core]
        pair(k).wait_recv()
        c_src[p] = c_both[p].reshape(16, LANES).astype(BF16)

        @pl.loop(0, ny if k < nz - 1 else ny - 1)
        def _(i):
            to_chip(2, c_src.at[p], c_dst, p, plane(i)).start()

    scores = score(layer(0))
    for k in range(nz):
        ahead = score(layer(k + 1)) if k < nz - 1 else None
        attend(layer(k), scores)
        scores = ahead
        pair(k).start()
        if k > 0:
            finish(k - 1)
    finish(nz - 1)
    c_dst[chip] = c_src[z]

    loads[7].wait()
    wait_all(recv_far.at[2], c_dst)
    third, summed = reduce(6, project_out, c_dst, d_give, d_take, d_src, d_dst)
    for j in range(per):
        rows[pl.ds(j, ny, stride=per), :] = summed[:, j, :]
    out_ref[...] = (wide[...] + rows[...]).astype(BF16)

    first.wait_send()
    second.wait_send()
    third.wait_send()
    for k in range(nz):
        pair(k).wait_send()
    wait_all(send_far.at[0], a_dst)
    wait_all(send_far.at[1], b_dst)
    wait_all(send_far.at[2], c_dst)
    wait_all(send_far.at[6], d_dst)


def body(
    nx,
    ny,
    hidden_in,
    norm_gain,
    w_query,
    key_weight,
    value_weight,
    w_output,
    key_cache_units,
    value_cache_units,
    key_scale,
    value_block_scale,
    lengths,
):
    width = hidden_in.shape[1]
    chunks = width // LANES
    depth, query_cols = w_query.shape
    key_cols = key_weight.shape[1]
    slots, cache_cols = key_cache_units.shape[1:]
    blocks = key_scale.shape[1]
    cols = query_cols + 2 * key_cols
    nz = nx // 2
    chips = nz * ny
    any_space = pl.BlockSpec(memory_space=pl.ANY)
    smem = pl.BlockSpec(memory_space=pltpu.SMEM)
    vmem = pltpu.VMEM
    out = pl.pallas_call(
        functools.partial(kernel, nz, ny),
        out_shape=jax.ShapeDtypeStruct((chunks, LANES), BF16),
        in_specs=[any_space] * 8 + [smem] * 3,
        out_specs=pl.BlockSpec(memory_space=pltpu.VMEM),
        scratch_shapes=[
            vmem((1, width), BF16),
            vmem((chunks, LANES), F32),
            vmem((depth, query_cols), BF16),
            vmem((2 * key_cols, depth), BF16),
            vmem((depth, query_cols), BF16),
            vmem((slots, cache_cols), BF16),
            vmem((slots, cache_cols), BF16),
            vmem((chunks, LANES), F32),
            vmem((nz, 2, 8, LANES), F32),
            vmem((nz, 2, 8, LANES), F32),
            vmem((nz, 16, LANES), BF16),
            vmem((chips, 16, LANES), BF16),
            vmem((chips * 16, LANES), F32),
            vmem((chips, cols), F32),
            vmem((chips, cols), F32),
            vmem((chips, cols // LANES, LANES), F32),
            vmem((chips, cols // LANES, LANES), F32),
            vmem((ny, 8, LANES), F32),
            vmem((chunks, LANES), F32),
            vmem((chunks, LANES), F32),
            vmem((chunks, slots), F32),
            vmem((chunks, slots), F32),
            vmem((nz, 2, 8, LANES), F32),
            vmem((nz, 2, 8, LANES), F32),
            vmem((nz, 16, LANES), BF16),
            vmem((chips, 16, LANES), BF16),
            vmem((chips, query_cols), F32),
            vmem((chips, query_cols), F32),
            vmem((chips, query_cols // LANES, LANES), F32),
            vmem((chips, query_cols // LANES, LANES), F32),
            pltpu.SemaphoreType.DMA((8,)),
            pltpu.SemaphoreType.DMA((7,)),
            pltpu.SemaphoreType.DMA((7,)),
            pltpu.SemaphoreType.DMA((7,)),
            pltpu.SemaphoreType.DMA((7,)),
            pltpu.SemaphoreType.REGULAR,
        ],
        compiler_params=pltpu.CompilerParams(
            collective_id=0, has_side_effects=True, vmem_limit_bytes=63 * 1024 * 1024
        ),
    )(
        hidden_in,
        norm_gain.reshape(chunks, LANES),
        w_query,
        key_weight.T,
        value_weight.T,
        w_output,
        key_cache_units.reshape(slots, cache_cols),
        value_cache_units.reshape(slots, cache_cols),
        key_scale.reshape(blocks, GROUPS).T,
        value_block_scale.reshape(blocks, GROUPS).T,
        lengths,
    )
    return out.reshape(1, width)


def solution(mesh):
    placed = (
        P(("gx", "gy"), None),
        P(),
        P("gx", "gy"),
        P("gx", "gy"),
        P("gx", "gy"),
        P("gx", "gy"),
        P(("gx", "gy"), None, None),
        P(("gx", "gy"), None, None),
        P(("gx", "gy"), None, None),
        P(("gx", "gy"), None, None),
        P(("gx", "gy")),
    )
    return jax.shard_map(
        functools.partial(body, mesh.shape["gx"], mesh.shape["gy"]),
        mesh=mesh,
        in_specs=placed,
        out_specs=P(("gx", "gy"), None),
        check_vma=False,
    )
```

```python
import functools
import math

import jax
import jax.numpy as jnp
from jax import lax
from jax.experimental import pallas as pl
from jax.experimental.pallas import tpu as pltpu
from jax.sharding import PartitionSpec as P

MESH = pl.DeviceIdType.MESH
F32 = jnp.float32
BF16 = jnp.bfloat16

GROUPS = 8
LANES = 128
ROPE_BASE = 500000.0
NORM_EPS = 1e-05
MASKED_SCORE = -1e30


def kernel(
    nz,
    ny,
    hidden_hbm,
    gain_hbm,
    wq_hbm,
    wk_hbm,
    wv_hbm,
    wo_hbm,
    keys_hbm,
    values_hbm,
    key_scale_hbm,
    value_scale_hbm,
    lengths,
    out_ref,
    hidden,
    gain,
    wq,
    wkv,
    wo,
    keys,
    values,
    wide,
    normed,
    a_both,
    a_src,
    a_dst,
    spare,
    b_give,
    b_take,
    b_src,
    b_dst,
    heads_in,
    rows,
    queries,
    kscale,
    vscale,
    mixed_out,
    c_both,
    c_src,
    c_dst,
    d_give,
    d_take,
    d_src,
    d_dst,
    key_scale,
    value_scale,
    load_sem,
    send_core,
    recv_core,
    send_far,
    recv_far,
    plane_in,
):
    gx = lax.axis_index("gx")
    gy = lax.axis_index("gy")
    z, core = gx // 2, lax.rem(gx, 2)
    other = 1 - core
    side = 4
    px, py = gy // side, lax.rem(gy, side)
    chips = nz * ny
    chip = z * ny + gy
    slots = keys.shape[0]
    blocks = slots // LANES

    key_cols = wk_hbm.shape[0]
    loads = [
        pltpu.make_async_copy(src, dst, load_sem.at[i])
        for i, (src, dst) in enumerate(
            (
                (hidden_hbm, hidden),
                (gain_hbm, gain),
                (wk_hbm, wkv.at[pl.ds(0, key_cols)]),
                (wv_hbm, wkv.at[pl.ds(key_cols, key_cols)]),
                (wq_hbm, wq),
                (keys_hbm, keys),
                (values_hbm, values),
                (wo_hbm, wo),
                (key_scale_hbm, key_scale),
                (value_scale_hbm, value_scale),
            )
        )
    ]
    loads[0].start()
    loads[1].start()

    def away(i):
        return jnp.where(i == 3, 0, jnp.where(i == 2, 3, 2 - i))

    def plane(i):
        return lax.rem(px + away(i // side), side) * side + lax.rem(
            py + away(lax.rem(i, side)), side
        )

    def layer(i):
        return lax.rem(z + away(i), nz)

    barrier = pltpu.get_barrier_semaphore()

    @pl.loop(0, ny - 1)
    def _(i):
        pl.semaphore_signal(barrier, inc=1, device_id=(gx, plane(i)), device_id_type=MESH)

    for i in range(nz - 1):
        pl.semaphore_signal(
            barrier, inc=1, device_id=(layer(i) * 2 + core, gy), device_id_type=MESH
        )
    pl.semaphore_signal(barrier, inc=1, device_id=(z * 2 + other, gy), device_id_type=MESH)

    for load in loads[8:] + loads[2:8]:
        load.start()

    def to_core(i, src, dst):
        return pltpu.make_async_remote_copy(
            src_ref=src,
            dst_ref=dst,
            send_sem=send_core.at[i],
            recv_sem=recv_core.at[i],
            device_id=(z * 2 + other, gy),
            device_id_type=MESH,
        )

    def to_chip(i, src, dst, tz, ty):
        return pltpu.make_async_remote_copy(
            src_ref=src,
            dst_ref=dst.at[chip],
            send_sem=send_far.at[i],
            recv_sem=recv_far.at[i],
            device_id=(tz * 2 + core, ty),
            device_id_type=MESH,
        )

    def to_all(i, src, dst):
        @pl.loop(0, chips - 1)
        def _(k):
            tz, ty = layer(k // ny), plane(lax.rem(k, ny))
            to_chip(i, src(tz, ty), dst, tz, ty).start()

    def wait_all(sem, ref):
        most = ref.at[pl.ds(0, chips - 1)]
        pltpu.make_async_copy(most, most, sem).wait()

    loads[0].wait()
    row = hidden[...].astype(F32)
    for s in range(wide.shape[0]):
        wide[s : s + 1, :] = row[:, s * LANES : (s + 1) * LANES]
    loads[1].wait()
    x = wide[...]
    variance = jnp.sum(jnp.sum(x * x, axis=0, keepdims=True), axis=1, keepdims=True) * (
        1.0 / (x.shape[0] * LANES)
    )
    x = (x * lax.rsqrt(variance + NORM_EPS) * gain[...]).astype(BF16).astype(F32)
    normed[...] = x.reshape(normed.shape)

    pl.semaphore_wait(barrier, ny + nz - 1)
    for i in range(nz - 1):
        pl.semaphore_signal(
            plane_in, inc=1, device_id=(layer(i) * 2 + core, gy), device_id_type=MESH
        )

    first = to_core(0, normed.at[:, other], a_both.at[:, core])
    first.start()
    for t in range(nz):
        a_both[t, core] = normed[t, core]

    length = lengths[0]
    lane = lax.broadcasted_iota(jnp.int32, (1, LANES), 1)
    step = (lane % 64).astype(F32)
    angle = length.astype(F32) * jnp.exp(step * (-2.0 * math.log(ROPE_BASE) / LANES))
    inv_root = 1.0 / math.sqrt(LANES)

    first.wait_recv()
    a_src[...] = a_both[...].reshape(a_src.shape).astype(BF16)

    @pl.loop(0, ny - 1)
    def _(i):
        to_chip(0, a_src.at[z], a_dst, z, plane(i)).start()

    pl.semaphore_wait(plane_in, nz - 1)

    @pl.loop(0, (nz - 1) * ny)
    def _(k):
        tz = layer(k // ny)
        to_chip(0, a_src.at[tz], a_dst, tz, plane(lax.rem(k, ny))).start()

    a_dst[chip] = a_src[z]

    cosine = jnp.cos(angle)
    sine = jnp.sin(angle)
    sine = jnp.where(lane < 64, -sine, sine)

    loads[8].wait()
    loads[9].wait()

    @pl.loop(0, blocks)
    def _(b):
        at = pl.ds(pl.multiple_of(b * LANES, LANES), LANES)
        for g in range(GROUPS):
            kscale[8 * g : 8 * g + 8, at] = jnp.full((8, LANES), key_scale[g, b] * inv_root, F32)
            vscale[8 * g : 8 * g + 8, at] = jnp.full((8, LANES), value_scale[g, b], F32)

    loads[2].wait()
    loads[3].wait()
    loads[4].wait()

    def requests(r):
        chunks = [spare[pl.ds(r * 8 + s, chips, stride=16), :] for s in range(8)]
        return jnp.concatenate(chunks, axis=1).astype(BF16)

    nt = (((1,), (1,)), ((), ()))

    def project(r):
        lhs = requests(r)
        return jnp.concatenate(
            [
                jnp.dot(lhs, wq[...], preferred_element_type=F32),
                lax.dot_general(lhs, wkv[...], nt, preferred_element_type=F32),
            ],
            axis=1,
        )

    def project_out(r):
        return jnp.dot(requests(r), wo[...], preferred_element_type=F32)

    def reduce(i, product, arrived, give, take, src, dst):
        spare[...] = arrived[...].astype(F32).reshape(spare.shape)
        give[...] = product(other)
        swap = to_core(i, give, take)
        swap.start()
        kept = product(core)
        swap.wait_recv()
        total = kept + take[...]
        for c in range(total.shape[1] // LANES):
            src[:, c, :] = total[:, c * LANES : (c + 1) * LANES]
        to_all(i, lambda tz, ty: src.at[tz * ny + ty], dst)
        dst[chip] = src[chip]
        wait_all(recv_far.at[i], dst)
        summed = dst[0:ny]
        for t in range(1, nz):
            summed = summed + dst[t * ny : (t + 1) * ny]
        return swap, summed

    wait_all(recv_far.at[0], a_dst)
    second, summed = reduce(1, project, a_dst, b_give, b_take, b_src, b_dst)
    heads_in[:, 0 : summed.shape[1], :] = summed.astype(BF16).astype(F32)

    per = wq.shape[1] // LANES
    for j in range(per):
        rows[pl.ds(j, ny, stride=per), :] = heads_in[:, j, :]
    both = heads_in[:, per, :]
    queries[0:ny, :] = both
    even = queries[pl.ds(0, ny // 2, stride=2), :]
    odd = queries[pl.ds(1, ny // 2, stride=2), :]
    front = lane < 64
    new_key = jnp.where(front, even, pltpu.roll(odd, 64, 1))
    new_value = jnp.where(front, pltpu.roll(even, 64, 1), odd)

    def rotate(v):
        return (v * cosine + pltpu.roll(v, 64, 1) * sine).astype(BF16).astype(F32)

    heads_in[0, :, :] = rotate(new_key)
    heads_in[1, :, :] = new_value
    queries[...] = rotate(rows[...])

    loads[5].wait()
    loads[6].wait()
    top = lax.broadcasted_iota(jnp.int32, (16, LANES), 0) < 8
    live = lax.broadcasted_iota(jnp.int32, (1, slots), 1) < length

    def score(p):
        cols = pl.ds(pl.multiple_of(2 * p * LANES, 2 * LANES), 2 * LANES)
        heads = pl.ds(pl.multiple_of(16 * p, 16), 16)
        q = queries[heads, :]
        spread_q = jnp.concatenate([jnp.where(top, q, 0.0), jnp.where(top, 0.0, q)], axis=1)
        scores = lax.dot_general(
            spread_q.astype(BF16), keys[:, cols], nt, preferred_element_type=F32
        )
        return jnp.where(live, scores * kscale[heads, :], MASKED_SCORE)

    def attend(p, scores):
        cols = pl.ds(pl.multiple_of(2 * p * LANES, 2 * LANES), 2 * LANES)
        heads = pl.ds(pl.multiple_of(16 * p, 16), 16)
        q = queries[heads, :]
        own_key = jnp.where(
            top, heads_in[0, pl.ds(2 * p, 1), :], heads_in[0, pl.ds(2 * p + 1, 1), :]
        )
        own_value = jnp.where(
            top, heads_in[1, pl.ds(2 * p, 1), :], heads_in[1, pl.ds(2 * p + 1, 1), :]
        )
        own_score = jnp.sum(q * own_key, axis=1, keepdims=True) * inv_root
        peak = jnp.maximum(jnp.max(scores, axis=1, keepdims=True), own_score)
        probs = jnp.exp(scores - peak)
        own_prob = jnp.exp(own_score - peak)
        total = jnp.sum(probs, axis=1, keepdims=True) + own_prob
        weighted = (probs * vscale[heads, :]).astype(BF16)
        mixed = jnp.dot(weighted, values[:, cols], preferred_element_type=F32)
        mixed = jnp.where(top, mixed[:, :LANES], mixed[:, LANES:])
        mixed = mixed + own_prob.astype(BF16).astype(F32) * own_value
        mixed = (mixed / total).astype(BF16).astype(F32)
        mixed_out[p] = mixed.reshape(2, 8, LANES)

    def pair(k):
        p = layer(k)
        return to_core(2 + k, mixed_out.at[p, other], c_both.at[p, core])

    def finish(k):
        p = layer(k)
        c_both[p, core] = mixed_out[p, core]
        pair(k).wait_recv()
        c_src[p] = c_both[p].reshape(16, LANES).astype(BF16)

        @pl.loop(0, ny if k < nz - 1 else ny - 1)
        def _(i):
            to_chip(2, c_src.at[p], c_dst, p, plane(i)).start()

    scores = score(layer(0))
    for k in range(nz):
        ahead = score(layer(k + 1)) if k < nz - 1 else None
        attend(layer(k), scores)
        scores = ahead
        pair(k).start()
        if k > 0:
            finish(k - 1)
    finish(nz - 1)
    c_dst[chip] = c_src[z]

    loads[7].wait()
    wait_all(recv_far.at[2], c_dst)
    third, summed = reduce(6, project_out, c_dst, d_give, d_take, d_src, d_dst)
    for j in range(per):
        rows[pl.ds(j, ny, stride=per), :] = summed[:, j, :]
    out_ref[...] = (wide[...] + rows[...]).astype(BF16)

    first.wait_send()
    second.wait_send()
    third.wait_send()
    for k in range(nz):
        pair(k).wait_send()
    wait_all(send_far.at[0], a_dst)
    wait_all(send_far.at[1], b_dst)
    wait_all(send_far.at[2], c_dst)
    wait_all(send_far.at[6], d_dst)


def body(
    nx,
    ny,
    hidden_in,
    norm_gain,
    w_query,
    key_weight,
    value_weight,
    w_output,
    key_cache_units,
    value_cache_units,
    key_scale,
    value_block_scale,
    lengths,
):
    width = hidden_in.shape[1]
    chunks = width // LANES
    depth, query_cols = w_query.shape
    key_cols = key_weight.shape[1]
    slots, cache_cols = key_cache_units.shape[1:]
    blocks = key_scale.shape[1]
    cols = query_cols + 2 * key_cols
    nz = nx // 2
    chips = nz * ny
    hbm = pl.BlockSpec(memory_space=pltpu.HBM)
    vmem = pltpu.VMEM
    out = pl.pallas_call(
        functools.partial(kernel, nz, ny),
        out_shape=jax.ShapeDtypeStruct((chunks, LANES), BF16),
        in_specs=[hbm] * 10 + [pl.BlockSpec(memory_space=pltpu.SMEM)],
        out_specs=pl.BlockSpec(memory_space=pltpu.VMEM),
        scratch_shapes=[
            vmem((1, width), BF16),
            vmem((chunks, LANES), F32),
            vmem((depth, query_cols), BF16),
            vmem((2 * key_cols, depth), BF16),
            vmem((depth, query_cols), BF16),
            vmem((slots, cache_cols), BF16),
            vmem((slots, cache_cols), BF16),
            vmem((chunks, LANES), F32),
            vmem((nz, 2, 8, LANES), F32),
            vmem((nz, 2, 8, LANES), F32),
            vmem((nz, 16, LANES), BF16),
            vmem((chips, 16, LANES), BF16),
            vmem((chips * 16, LANES), F32),
            vmem((chips, cols), F32),
            vmem((chips, cols), F32),
            vmem((chips, cols // LANES, LANES), F32),
            vmem((chips, cols // LANES, LANES), F32),
            vmem((ny, 8, LANES), F32),
            vmem((chunks, LANES), F32),
            vmem((chunks, LANES), F32),
            vmem((chunks, slots), F32),
            vmem((chunks, slots), F32),
            vmem((nz, 2, 8, LANES), F32),
            vmem((nz, 2, 8, LANES), F32),
            vmem((nz, 16, LANES), BF16),
            vmem((chips, 16, LANES), BF16),
            vmem((chips, query_cols), F32),
            vmem((chips, query_cols), F32),
            vmem((chips, query_cols // LANES, LANES), F32),
            vmem((chips, query_cols // LANES, LANES), F32),
            pltpu.SMEM((GROUPS, blocks), F32),
            pltpu.SMEM((GROUPS, blocks), F32),
            pltpu.SemaphoreType.DMA((10,)),
            pltpu.SemaphoreType.DMA((7,)),
            pltpu.SemaphoreType.DMA((7,)),
            pltpu.SemaphoreType.DMA((7,)),
            pltpu.SemaphoreType.DMA((7,)),
            pltpu.SemaphoreType.REGULAR,
        ],
        compiler_params=pltpu.CompilerParams(
            collective_id=0, has_side_effects=True, vmem_limit_bytes=32 * 1024 * 1024
        ),
    )(
        *(
            pltpu.with_memory_space_constraint(array, pltpu.HBM)
            for array in (
                hidden_in,
                norm_gain.reshape(chunks, LANES),
                w_query,
                key_weight.T,
                value_weight.T,
                w_output,
                key_cache_units.reshape(slots, cache_cols),
                value_cache_units.reshape(slots, cache_cols),
                key_scale.reshape(blocks, GROUPS).T,
                value_block_scale.reshape(blocks, GROUPS).T,
            )
        ),
        lengths,
    )
    return out.reshape(1, width)


def solution(mesh):
    placed = (
        P(("gx", "gy"), None),
        P(),
        P("gx", "gy"),
        P("gx", "gy"),
        P("gx", "gy"),
        P("gx", "gy"),
        P(("gx", "gy"), None, None),
        P(("gx", "gy"), None, None),
        P(("gx", "gy"), None, None),
        P(("gx", "gy"), None, None),
        P(("gx", "gy")),
    )
    return jax.shard_map(
        functools.partial(body, mesh.shape["gx"], mesh.shape["gy"]),
        mesh=mesh,
        in_specs=placed,
        out_specs=P(("gx", "gy"), None),
        check_vma=False,
    )
```

```python
import functools
import math

import jax
import jax.numpy as jnp
from jax import lax
from jax.experimental import pallas as pl
from jax.experimental.pallas import tpu as pltpu
from jax.sharding import PartitionSpec as P

MESH = pl.DeviceIdType.MESH
F32 = jnp.float32
BF16 = jnp.bfloat16

GROUPS = 8
LANES = 128
ROPE_BASE = 500000.0
NORM_EPS = 1e-05
MASKED_SCORE = -1e30


def kernel(
    nz,
    ny,
    hidden_hbm,
    gain_hbm,
    wq_hbm,
    wk_hbm,
    wv_hbm,
    wo_hbm,
    keys_hbm,
    values_hbm,
    key_scale_hbm,
    value_scale_hbm,
    lengths,
    out_ref,
    hidden,
    gain,
    wq,
    wkv,
    wo,
    keys,
    values,
    wide,
    normed,
    a_both,
    a_src,
    a_dst,
    spare,
    b_give,
    b_take,
    b_src,
    b_dst,
    heads_in,
    rows,
    queries,
    kscale,
    vscale,
    c_src,
    c_dst,
    d_give,
    d_take,
    d_src,
    d_dst,
    key_scale,
    value_scale,
    load_sem,
    send_core,
    recv_core,
    send_far,
    recv_far,
    plane_in,
):
    gx = lax.axis_index("gx")
    gy = lax.axis_index("gy")
    z, core = gx // 2, lax.rem(gx, 2)
    other = 1 - core
    side = 4
    px, py = gy // side, lax.rem(gy, side)
    chips = nz * ny
    chip = z * ny + gy
    slots = keys.shape[0]
    blocks = slots // LANES

    key_cols = wk_hbm.shape[0]
    loads = [
        pltpu.make_async_copy(src, dst, load_sem.at[i])
        for i, (src, dst) in enumerate(
            (
                (hidden_hbm, hidden),
                (gain_hbm, gain),
                (wk_hbm, wkv.at[pl.ds(0, key_cols)]),
                (wv_hbm, wkv.at[pl.ds(key_cols, key_cols)]),
                (wq_hbm, wq),
                (keys_hbm, keys),
                (values_hbm, values),
                (wo_hbm, wo),
                (key_scale_hbm, key_scale),
                (value_scale_hbm, value_scale),
            )
        )
    ]
    loads[0].start()
    loads[1].start()

    steps = (0, 1, 2, 3)
    hops = (0, 1, 2, 1)
    along_z = [lax.rem(z + d, nz) for d in steps]
    along_x = [lax.rem(px + d, side) * side for d in steps]
    along_y = [lax.rem(py + d, side) for d in steps]

    def by_distance(layers):
        return sorted(
            ((a, b, c) for a in layers for b in steps for c in steps if (a, b, c) != (0, 0, 0)),
            key=lambda d: (-hops[d[0]] - hops[d[1]] - hops[d[2]], d),
        )

    def plane(d):
        return along_x[d[1]] + along_y[d[2]]

    barrier = pltpu.get_barrier_semaphore()

    for d in by_distance((0,)):
        pl.semaphore_signal(barrier, inc=1, device_id=(gx, plane(d)), device_id_type=MESH)
    for tz in (along_z[2], along_z[1], along_z[3]):
        pl.semaphore_signal(barrier, inc=1, device_id=(tz * 2 + core, gy), device_id_type=MESH)
    pl.semaphore_signal(barrier, inc=1, device_id=(z * 2 + other, gy), device_id_type=MESH)

    for load in loads[8:] + loads[2:8]:
        load.start()

    def to_core(i, src, dst):
        return pltpu.make_async_remote_copy(
            src_ref=src,
            dst_ref=dst,
            send_sem=send_core.at[i],
            recv_sem=recv_core.at[i],
            device_id=(z * 2 + other, gy),
            device_id_type=MESH,
        )

    def to_chip(i, src, dst, tz, ty):
        return pltpu.make_async_remote_copy(
            src_ref=src,
            dst_ref=dst.at[chip],
            send_sem=send_far.at[i],
            recv_sem=recv_far.at[i],
            device_id=(tz * 2 + core, ty),
            device_id_type=MESH,
        )

    def to_all(i, src, dst):
        for d in by_distance(steps):
            tz, ty = along_z[d[0]], plane(d)
            to_chip(i, src(tz, ty), dst, tz, ty).start()

    def wait_all(sem, ref):
        most = ref.at[pl.ds(0, ref.shape[0] - 1)]
        pltpu.make_async_copy(most, most, sem).wait()

    loads[0].wait()
    row = hidden[...].astype(F32)
    for s in range(wide.shape[0]):
        wide[s : s + 1, :] = row[:, s * LANES : (s + 1) * LANES]
    loads[1].wait()
    x = wide[...]
    variance = jnp.sum(jnp.sum(x * x, axis=0, keepdims=True), axis=1, keepdims=True) * (
        1.0 / (x.shape[0] * LANES)
    )
    x = (x * lax.rsqrt(variance + NORM_EPS) * gain[...]).astype(BF16).astype(F32)
    normed[...] = x.reshape(normed.shape)

    pl.semaphore_wait(barrier, ny + nz - 1)
    for tz in (along_z[2], along_z[1], along_z[3]):
        pl.semaphore_signal(plane_in, inc=1, device_id=(tz * 2 + core, gy), device_id_type=MESH)

    first = to_core(0, normed.at[:, other], a_both.at[:, core])
    first.start()
    for t in range(nz):
        a_both[t, core] = normed[t, core]

    length = lengths[0]
    lane = lax.broadcasted_iota(jnp.int32, (1, LANES), 1)
    step = (lane % 64).astype(F32)
    angle = length.astype(F32) * jnp.exp(step * (-2.0 * math.log(ROPE_BASE) / LANES))
    inv_root = 1.0 / math.sqrt(LANES)

    first.wait_recv()
    a_src[...] = a_both[...].reshape(a_src.shape).astype(BF16)
    for d in by_distance((0,)):
        to_chip(0, a_src.at[z], a_dst, z, plane(d)).start()
    pl.semaphore_wait(plane_in, nz - 1)
    for d in by_distance((1, 2, 3)):
        tz = along_z[d[0]]
        to_chip(0, a_src.at[tz], a_dst, tz, plane(d)).start()
    a_dst[chip] = a_src[z]

    cosine = jnp.cos(angle)
    sine = jnp.sin(angle)
    sine = jnp.where(lane < 64, -sine, sine)

    loads[8].wait()
    loads[9].wait()

    @pl.loop(0, blocks)
    def _(b):
        at = pl.ds(pl.multiple_of(b * LANES, LANES), LANES)
        for g in range(GROUPS):
            kscale[8 * g : 8 * g + 8, at] = jnp.full((8, LANES), key_scale[g, b] * inv_root, F32)
            vscale[8 * g : 8 * g + 8, at] = jnp.full((8, LANES), value_scale[g, b], F32)

    loads[2].wait()
    loads[3].wait()
    loads[4].wait()

    def requests(start, stride):
        chunks = [spare[pl.ds(start + s, chips, stride=stride), :] for s in range(8)]
        return jnp.concatenate(chunks, axis=1).astype(BF16)

    nt = (((1,), (1,)), ((), ()))

    def project(r):
        lhs = requests(r * 8, 16)
        return jnp.concatenate(
            [
                jnp.dot(lhs, wq[...], preferred_element_type=F32),
                lax.dot_general(lhs, wkv[...], nt, preferred_element_type=F32),
            ],
            axis=1,
        )

    def project_out(r):
        return jnp.dot(requests(r * 8 * chips, 8), wo[...], preferred_element_type=F32)

    def reduce(i, product, arrived, give, take, src, dst):
        spare[...] = arrived[...].astype(F32).reshape(spare.shape)
        give[...] = product(other)
        swap = to_core(i, give, take)
        swap.start()
        kept = product(core)
        swap.wait_recv()
        total = kept + take[...]
        for c in range(total.shape[1] // LANES):
            src[:, c, :] = total[:, c * LANES : (c + 1) * LANES]
        to_all(i, lambda tz, ty: src.at[tz * ny + ty], dst)
        dst[chip] = src[chip]
        wait_all(recv_far.at[i], dst)
        summed = dst[0:ny]
        for t in range(1, nz):
            summed = summed + dst[t * ny : (t + 1) * ny]
        return swap, summed

    wait_all(recv_far.at[0], a_dst)
    second, summed = reduce(1, project, a_dst, b_give, b_take, b_src, b_dst)
    heads_in[:, 0 : summed.shape[1], :] = summed.astype(BF16).astype(F32)

    per = wq.shape[1] // LANES
    for j in range(per):
        rows[pl.ds(j, ny, stride=per), :] = heads_in[:, j, :]
    both = heads_in[:, per, :]
    queries[0:ny, :] = both
    even = queries[pl.ds(0, ny // 2, stride=2), :]
    odd = queries[pl.ds(1, ny // 2, stride=2), :]
    front = lane < 64
    new_key = jnp.where(front, even, pltpu.roll(odd, 64, 1))
    new_value = jnp.where(front, pltpu.roll(even, 64, 1), odd)

    def rotate(v):
        return (v * cosine + pltpu.roll(v, 64, 1) * sine).astype(BF16).astype(F32)

    heads_in[0, :, :] = rotate(new_key)
    heads_in[1, :, :] = new_value
    queries[...] = rotate(rows[...])

    loads[5].wait()
    loads[6].wait()
    top = lax.broadcasted_iota(jnp.int32, (16, LANES), 0) < 8
    live = lax.broadcasted_iota(jnp.int32, (1, slots), 1) < length

    def score(p):
        cols = pl.ds(pl.multiple_of(2 * p * LANES, 2 * LANES), 2 * LANES)
        heads = pl.ds(pl.multiple_of(16 * p, 16), 16)
        q = queries[heads, :]
        spread_q = jnp.concatenate([jnp.where(top, q, 0.0), jnp.where(top, 0.0, q)], axis=1)
        scores = lax.dot_general(
            spread_q.astype(BF16), keys[:, cols], nt, preferred_element_type=F32
        )
        return jnp.where(live, scores * kscale[heads, :], MASKED_SCORE)

    def attend(p, scores):
        cols = pl.ds(pl.multiple_of(2 * p * LANES, 2 * LANES), 2 * LANES)
        heads = pl.ds(pl.multiple_of(16 * p, 16), 16)
        q = queries[heads, :]
        own_key = jnp.where(
            top, heads_in[0, pl.ds(2 * p, 1), :], heads_in[0, pl.ds(2 * p + 1, 1), :]
        )
        own_value = jnp.where(
            top, heads_in[1, pl.ds(2 * p, 1), :], heads_in[1, pl.ds(2 * p + 1, 1), :]
        )
        own_score = jnp.sum(q * own_key, axis=1, keepdims=True) * inv_root
        peak = jnp.maximum(jnp.max(scores, axis=1, keepdims=True), own_score)
        probs = jnp.exp(scores - peak)
        own_prob = jnp.exp(own_score - peak)
        total = jnp.sum(probs, axis=1, keepdims=True) + own_prob
        weighted = (probs * vscale[heads, :]).astype(BF16)
        mixed = jnp.dot(weighted, values[:, cols], preferred_element_type=F32)
        mixed = jnp.where(top, mixed[:, :LANES], mixed[:, LANES:])
        mixed = mixed + own_prob.astype(BF16).astype(F32) * own_value
        c_src[p] = (mixed / total).astype(BF16).reshape(2, 8, LANES)

    slot = core * chips + chip

    def send_heads(a):
        p = along_z[a]
        for d in by_distance((a,)):
            for half in (0, 1):
                pltpu.make_async_remote_copy(
                    src_ref=c_src.at[p, half],
                    dst_ref=c_dst.at[slot],
                    send_sem=send_far.at[2],
                    recv_sem=recv_far.at[2],
                    device_id=(p * 2 + half, plane(d)),
                    device_id_type=MESH,
                ).start()

    order = (2, 1, 3, 0)
    scores = score(along_z[order[0]])
    for k in range(nz):
        ahead = score(along_z[order[k + 1]]) if k < nz - 1 else None
        attend(along_z[order[k]], scores)
        scores = ahead
        send_heads(order[k])
    pltpu.make_async_remote_copy(
        src_ref=c_src.at[z, other],
        dst_ref=c_dst.at[slot],
        send_sem=send_far.at[2],
        recv_sem=recv_far.at[2],
        device_id=(z * 2 + other, gy),
        device_id_type=MESH,
    ).start()
    c_dst[slot] = c_src[z, core]

    loads[7].wait()
    wait_all(recv_far.at[2], c_dst)
    third, summed = reduce(3, project_out, c_dst, d_give, d_take, d_src, d_dst)
    for j in range(per):
        rows[pl.ds(j, ny, stride=per), :] = summed[:, j, :]
    out_ref[...] = (wide[...] + rows[...]).astype(BF16)

    first.wait_send()
    second.wait_send()
    third.wait_send()
    wait_all(send_far.at[0], a_dst)
    wait_all(send_far.at[1], b_dst)
    wait_all(send_far.at[2], c_dst)
    wait_all(send_far.at[3], d_dst)


def body(
    nx,
    ny,
    hidden_in,
    norm_gain,
    w_query,
    key_weight,
    value_weight,
    w_output,
    key_cache_units,
    value_cache_units,
    key_scale,
    value_block_scale,
    lengths,
):
    width = hidden_in.shape[1]
    chunks = width // LANES
    depth, query_cols = w_query.shape
    key_cols = key_weight.shape[1]
    slots, cache_cols = key_cache_units.shape[1:]
    blocks = key_scale.shape[1]
    cols = query_cols + 2 * key_cols
    nz = nx // 2
    chips = nz * ny
    hbm = pl.BlockSpec(memory_space=pltpu.HBM)
    vmem = pltpu.VMEM
    out = pl.pallas_call(
        functools.partial(kernel, nz, ny),
        out_shape=jax.ShapeDtypeStruct((chunks, LANES), BF16),
        in_specs=[hbm] * 10 + [pl.BlockSpec(memory_space=pltpu.SMEM)],
        out_specs=pl.BlockSpec(memory_space=pltpu.VMEM),
        scratch_shapes=[
            vmem((1, width), BF16),
            vmem((chunks, LANES), F32),
            vmem((depth, query_cols), BF16),
            vmem((2 * key_cols, depth), BF16),
            vmem((depth, query_cols), BF16),
            vmem((slots, cache_cols), BF16),
            vmem((slots, cache_cols), BF16),
            vmem((chunks, LANES), F32),
            vmem((nz, 2, 8, LANES), F32),
            vmem((nz, 2, 8, LANES), F32),
            vmem((nz, 16, LANES), BF16),
            vmem((chips, 16, LANES), BF16),
            vmem((chips * 16, LANES), F32),
            vmem((chips, cols), F32),
            vmem((chips, cols), F32),
            vmem((chips, cols // LANES, LANES), F32),
            vmem((chips, cols // LANES, LANES), F32),
            vmem((ny, 8, LANES), F32),
            vmem((chunks, LANES), F32),
            vmem((chunks, LANES), F32),
            vmem((chunks, slots), F32),
            vmem((chunks, slots), F32),
            vmem((nz, 2, 8, LANES), BF16),
            vmem((2 * chips, 8, LANES), BF16),
            vmem((chips, query_cols), F32),
            vmem((chips, query_cols), F32),
            vmem((chips, query_cols // LANES, LANES), F32),
            vmem((chips, query_cols // LANES, LANES), F32),
            pltpu.SMEM((GROUPS, blocks), F32),
            pltpu.SMEM((GROUPS, blocks), F32),
            pltpu.SemaphoreType.DMA((10,)),
            pltpu.SemaphoreType.DMA((4,)),
            pltpu.SemaphoreType.DMA((4,)),
            pltpu.SemaphoreType.DMA((4,)),
            pltpu.SemaphoreType.DMA((4,)),
            pltpu.SemaphoreType.REGULAR,
        ],
        compiler_params=pltpu.CompilerParams(
            collective_id=0, has_side_effects=True, vmem_limit_bytes=32 * 1024 * 1024
        ),
    )(
        *(
            pltpu.with_memory_space_constraint(array, pltpu.HBM)
            for array in (
                hidden_in,
                norm_gain.reshape(chunks, LANES),
                w_query,
                key_weight.T,
                value_weight.T,
                w_output,
                key_cache_units.reshape(slots, cache_cols),
                value_cache_units.reshape(slots, cache_cols),
                key_scale.reshape(blocks, GROUPS).T,
                value_block_scale.reshape(blocks, GROUPS).T,
            )
        ),
        lengths,
    )
    return out.reshape(1, width)


def solution(mesh):
    placed = (
        P(("gx", "gy"), None),
        P(),
        P("gx", "gy"),
        P("gx", "gy"),
        P("gx", "gy"),
        P("gx", "gy"),
        P(("gx", "gy"), None, None),
        P(("gx", "gy"), None, None),
        P(("gx", "gy"), None, None),
        P(("gx", "gy"), None, None),
        P(("gx", "gy")),
    )
    return jax.shard_map(
        functools.partial(body, mesh.shape["gx"], mesh.shape["gy"]),
        mesh=mesh,
        in_specs=placed,
        out_specs=P(("gx", "gy"), None),
        check_vma=False,
    )
```

```python
import functools
import math

import jax
import jax.numpy as jnp
from jax import lax
from jax.experimental import pallas as pl
from jax.experimental.pallas import tpu as pltpu
from jax.sharding import PartitionSpec as P

MESH = pl.DeviceIdType.MESH
F32 = jnp.float32
BF16 = jnp.bfloat16

GROUPS = 8
LANES = 128
ROPE_BASE = 500000.0
NORM_EPS = 1e-05
MASKED_SCORE = -1e30


def kernel(
    nz,
    ny,
    hidden_hbm,
    gain_hbm,
    wq_hbm,
    wk_hbm,
    wv_hbm,
    wo_hbm,
    keys_hbm,
    values_hbm,
    key_scale_hbm,
    value_scale_hbm,
    lengths,
    out_ref,
    hidden,
    gain,
    wq,
    wkv,
    wo,
    keys,
    values,
    wide,
    a_src,
    a_dst,
    spare,
    b_src,
    b_dst,
    heads_in,
    rows,
    queries,
    kscale,
    vscale,
    c_src,
    c_dst,
    d_src,
    d_dst,
    key_scale,
    value_scale,
    load_sem,
    send_core,
    recv_core,
    send_far,
    recv_far,
    plane_in,
):
    gx = lax.axis_index("gx")
    gy = lax.axis_index("gy")
    z, core = gx // 2, lax.rem(gx, 2)
    other = 1 - core
    side = 4
    px, py = gy // side, lax.rem(gy, side)
    chips = nz * ny
    chip = z * ny + gy
    slots = keys.shape[0]
    blocks = slots // LANES

    key_cols = wk_hbm.shape[0]
    loads = [
        pltpu.make_async_copy(src, dst, load_sem.at[i])
        for i, (src, dst) in enumerate(
            (
                (hidden_hbm, hidden),
                (gain_hbm, gain),
                (wk_hbm, wkv.at[core, pl.ds(0, key_cols)]),
                (wv_hbm, wkv.at[core, pl.ds(key_cols, key_cols)]),
                (wq_hbm, wq.at[core]),
                (keys_hbm, keys),
                (values_hbm, values),
                (wo_hbm, wo.at[core]),
                (key_scale_hbm, key_scale),
                (value_scale_hbm, value_scale),
            )
        )
    ]
    loads[0].start()
    loads[1].start()

    steps = (0, 1, 2, 3)
    hops = (0, 1, 2, 1)
    along_z = [lax.rem(z + d, nz) for d in steps]
    along_x = [lax.rem(px + d, side) * side for d in steps]
    along_y = [lax.rem(py + d, side) for d in steps]

    def by_distance(layers):
        return sorted(
            ((a, b, c) for a in layers for b in steps for c in steps if (a, b, c) != (0, 0, 0)),
            key=lambda d: (-hops[d[0]] - hops[d[1]] - hops[d[2]], d),
        )

    def plane(d):
        return along_x[d[1]] + along_y[d[2]]

    barrier = pltpu.get_barrier_semaphore()

    for d in by_distance((0,)):
        pl.semaphore_signal(barrier, inc=1, device_id=(gx, plane(d)), device_id_type=MESH)
    for tz in (along_z[2], along_z[1], along_z[3]):
        pl.semaphore_signal(barrier, inc=1, device_id=(tz * 2 + core, gy), device_id_type=MESH)
    pl.semaphore_signal(barrier, inc=1, device_id=(z * 2 + other, gy), device_id_type=MESH)

    for load in loads[8:] + loads[2:8]:
        load.start()

    def to_core(i, src, dst):
        return pltpu.make_async_remote_copy(
            src_ref=src,
            dst_ref=dst,
            send_sem=send_core.at[i],
            recv_sem=recv_core.at[i],
            device_id=(z * 2 + other, gy),
            device_id_type=MESH,
        )

    def to_chip(i, src, dst, tz, ty):
        return pltpu.make_async_remote_copy(
            src_ref=src,
            dst_ref=dst.at[chip],
            send_sem=send_far.at[i],
            recv_sem=recv_far.at[i],
            device_id=(tz * 2 + core, ty),
            device_id_type=MESH,
        )

    def to_all(i, src, dst):
        for d in by_distance(steps):
            tz, ty = along_z[d[0]], plane(d)
            to_chip(i, src(tz, ty), dst, tz, ty).start()

    def wait_all(sem, ref):
        most = ref.at[pl.ds(0, ref.shape[0] - 1)]
        pltpu.make_async_copy(most, most, sem).wait()

    loads[0].wait()
    row = hidden[...].astype(F32)
    for s in range(wide.shape[0]):
        wide[s : s + 1, :] = row[:, s * LANES : (s + 1) * LANES]
    loads[1].wait()
    x = wide[...]
    variance = jnp.sum(jnp.sum(x * x, axis=0, keepdims=True), axis=1, keepdims=True) * (
        1.0 / (x.shape[0] * LANES)
    )
    x = (x * lax.rsqrt(variance + NORM_EPS) * gain[...]).astype(BF16)
    a_src[...] = x.reshape(a_src.shape)

    pl.semaphore_wait(barrier, ny + nz - 1)
    for tz in (along_z[2], along_z[1], along_z[3]):
        pl.semaphore_signal(plane_in, inc=1, device_id=(tz * 2 + core, gy), device_id_type=MESH)

    for d in by_distance((0,)):
        to_chip(0, a_src.at[z], a_dst, z, plane(d)).start()
    pl.semaphore_wait(plane_in, nz - 1)
    for d in by_distance((1, 2, 3)):
        tz = along_z[d[0]]
        to_chip(0, a_src.at[tz], a_dst, tz, plane(d)).start()
    a_dst[chip] = a_src[z]

    shared = [
        to_core(0, wk_hbm, wkv.at[core, pl.ds(0, key_cols)]),
        to_core(1, wv_hbm, wkv.at[core, pl.ds(key_cols, key_cols)]),
        to_core(2, wq_hbm, wq.at[core]),
        to_core(3, wo_hbm, wo.at[core]),
    ]
    for share in shared:
        share.start()

    length = lengths[0]
    lane = lax.broadcasted_iota(jnp.int32, (1, LANES), 1)
    step = (lane % 64).astype(F32)
    angle = length.astype(F32) * jnp.exp(step * (-2.0 * math.log(ROPE_BASE) / LANES))
    inv_root = 1.0 / math.sqrt(LANES)

    cosine = jnp.cos(angle)
    sine = jnp.sin(angle)
    sine = jnp.where(lane < 64, -sine, sine)

    loads[8].wait()
    loads[9].wait()

    @pl.loop(0, blocks)
    def _(b):
        at = pl.ds(pl.multiple_of(b * LANES, LANES), LANES)
        for g in range(GROUPS):
            kscale[8 * g : 8 * g + 8, at] = jnp.full((8, LANES), key_scale[g, b] * inv_root, F32)
            vscale[8 * g : 8 * g + 8, at] = jnp.full((8, LANES), value_scale[g, b], F32)

    loads[2].wait()
    loads[3].wait()
    loads[4].wait()

    for share in shared[:3]:
        share.wait_recv()

    nt = (((1,), (1,)), ((), ()))

    def requests(arrived):
        spare[...] = arrived[...].astype(F32).reshape(spare.shape)
        chunks = [spare[pl.ds(s, chips, stride=16), :] for s in range(16)]
        return (
            jnp.concatenate(chunks[:8], axis=1).astype(BF16),
            jnp.concatenate(chunks[8:], axis=1).astype(BF16),
        )

    def product(low, high, weights):
        return jnp.dot(low, weights[0], preferred_element_type=F32) + jnp.dot(
            high, weights[1], preferred_element_type=F32
        )

    def product_nt(low, high, weights):
        return lax.dot_general(
            low, weights[0], nt, preferred_element_type=F32
        ) + lax.dot_general(high, weights[1], nt, preferred_element_type=F32)

    def reduce(i, parts, src, dst):
        at = 0
        for part in parts:
            for c in range(part.shape[1] // LANES):
                src[:, at, :] = part[:, c * LANES : (c + 1) * LANES]
                at += 1
        to_all(i, lambda tz, ty: src.at[tz * ny + ty], dst)
        dst[chip] = src[chip]
        wait_all(recv_far.at[i], dst)
        summed = dst[0:ny]
        for t in range(1, nz):
            summed = summed + dst[t * ny : (t + 1) * ny]
        return summed

    wait_all(recv_far.at[0], a_dst)
    low, high = requests(a_dst)
    summed = reduce(1, (product(low, high, wq), product_nt(low, high, wkv)), b_src, b_dst)
    heads_in[:, 0 : summed.shape[1], :] = summed.astype(BF16).astype(F32)

    per = wq.shape[2] // LANES
    for j in range(per):
        rows[pl.ds(j, ny, stride=per), :] = heads_in[:, j, :]
    both = heads_in[:, per, :]
    queries[0:ny, :] = both
    even = queries[pl.ds(0, ny // 2, stride=2), :]
    odd = queries[pl.ds(1, ny // 2, stride=2), :]
    front = lane < 64
    new_key = jnp.where(front, even, pltpu.roll(odd, 64, 1))
    new_value = jnp.where(front, pltpu.roll(even, 64, 1), odd)

    def rotate(v):
        return (v * cosine + pltpu.roll(v, 64, 1) * sine).astype(BF16).astype(F32)

    heads_in[0, :, :] = rotate(new_key)
    heads_in[1, :, :] = new_value
    queries[...] = rotate(rows[...])

    loads[5].wait()
    loads[6].wait()
    top = lax.broadcasted_iota(jnp.int32, (16, LANES), 0) < 8
    live = lax.broadcasted_iota(jnp.int32, (1, slots), 1) < length

    def score(p):
        cols = pl.ds(pl.multiple_of(2 * p * LANES, 2 * LANES), 2 * LANES)
        heads = pl.ds(pl.multiple_of(16 * p, 16), 16)
        q = queries[heads, :]
        spread_q = jnp.concatenate([jnp.where(top, q, 0.0), jnp.where(top, 0.0, q)], axis=1)
        scores = lax.dot_general(
            spread_q.astype(BF16), keys[:, cols], nt, preferred_element_type=F32
        )
        return jnp.where(live, scores * kscale[heads, :], MASKED_SCORE)

    def attend(p, scores):
        cols = pl.ds(pl.multiple_of(2 * p * LANES, 2 * LANES), 2 * LANES)
        heads = pl.ds(pl.multiple_of(16 * p, 16), 16)
        q = queries[heads, :]
        own_key = jnp.where(
            top, heads_in[0, pl.ds(2 * p, 1), :], heads_in[0, pl.ds(2 * p + 1, 1), :]
        )
        own_value = jnp.where(
            top, heads_in[1, pl.ds(2 * p, 1), :], heads_in[1, pl.ds(2 * p + 1, 1), :]
        )
        own_score = jnp.sum(q * own_key, axis=1, keepdims=True) * inv_root
        peak = jnp.maximum(jnp.max(scores, axis=1, keepdims=True), own_score)
        probs = jnp.exp(scores - peak)
        own_prob = jnp.exp(own_score - peak)
        total = jnp.sum(probs, axis=1, keepdims=True) + own_prob
        weighted = (probs * vscale[heads, :]).astype(BF16)
        mixed = jnp.dot(weighted, values[:, cols], preferred_element_type=F32)
        mixed = jnp.where(top, mixed[:, :LANES], mixed[:, LANES:])
        mixed = mixed + own_prob.astype(BF16).astype(F32) * own_value
        c_src[p] = (mixed / total).astype(BF16)

    def send_heads(a):
        p = along_z[a]
        for d in by_distance((a,)):
            to_chip(2, c_src.at[p], c_dst, p, plane(d)).start()

    order = (2, 1, 3, 0)
    scores = score(along_z[order[0]])
    for k in range(nz):
        ahead = score(along_z[order[k + 1]]) if k < nz - 1 else None
        attend(along_z[order[k]], scores)
        scores = ahead
        send_heads(order[k])
    c_dst[chip] = c_src[z]

    loads[7].wait()
    wait_all(recv_far.at[2], c_dst)
    shared[3].wait_recv()
    low, high = requests(c_dst)
    summed = reduce(3, (product(low, high, wo),), d_src, d_dst)
    for j in range(per):
        rows[pl.ds(j, ny, stride=per), :] = summed[:, j, :]
    out_ref[...] = (wide[...] + rows[...]).astype(BF16)

    for share in shared:
        share.wait_send()
    wait_all(send_far.at[0], a_dst)
    wait_all(send_far.at[1], b_dst)
    wait_all(send_far.at[2], c_dst)
    wait_all(send_far.at[3], d_dst)


def body(
    nx,
    ny,
    hidden_in,
    norm_gain,
    w_query,
    key_weight,
    value_weight,
    w_output,
    key_cache_units,
    value_cache_units,
    key_scale,
    value_block_scale,
    lengths,
):
    width = hidden_in.shape[1]
    chunks = width // LANES
    depth, query_cols = w_query.shape
    key_cols = key_weight.shape[1]
    slots, cache_cols = key_cache_units.shape[1:]
    blocks = key_scale.shape[1]
    cols = query_cols + 2 * key_cols
    nz = nx // 2
    chips = nz * ny
    hbm = pl.BlockSpec(memory_space=pltpu.HBM)
    vmem = pltpu.VMEM
    out = pl.pallas_call(
        functools.partial(kernel, nz, ny),
        out_shape=jax.ShapeDtypeStruct((chunks, LANES), BF16),
        in_specs=[hbm] * 10 + [pl.BlockSpec(memory_space=pltpu.SMEM)],
        out_specs=pl.BlockSpec(memory_space=pltpu.VMEM),
        scratch_shapes=[
            vmem((1, width), BF16),
            vmem((chunks, LANES), F32),
            vmem((2, depth, query_cols), BF16),
            vmem((2, 2 * key_cols, depth), BF16),
            vmem((2, depth, query_cols), BF16),
            vmem((slots, cache_cols), BF16),
            vmem((slots, cache_cols), BF16),
            vmem((chunks, LANES), F32),
            vmem((nz, 16, LANES), BF16),
            vmem((chips, 16, LANES), BF16),
            vmem((chips * 16, LANES), F32),
            vmem((chips, cols // LANES, LANES), F32),
            vmem((chips, cols // LANES, LANES), F32),
            vmem((ny, 8, LANES), F32),
            vmem((chunks, LANES), F32),
            vmem((chunks, LANES), F32),
            vmem((chunks, slots), F32),
            vmem((chunks, slots), F32),
            vmem((nz, 16, LANES), BF16),
            vmem((chips, 16, LANES), BF16),
            vmem((chips, query_cols // LANES, LANES), F32),
            vmem((chips, query_cols // LANES, LANES), F32),
            pltpu.SMEM((GROUPS, blocks), F32),
            pltpu.SMEM((GROUPS, blocks), F32),
            pltpu.SemaphoreType.DMA((10,)),
            pltpu.SemaphoreType.DMA((4,)),
            pltpu.SemaphoreType.DMA((4,)),
            pltpu.SemaphoreType.DMA((4,)),
            pltpu.SemaphoreType.DMA((4,)),
            pltpu.SemaphoreType.REGULAR,
        ],
        compiler_params=pltpu.CompilerParams(
            collective_id=0, has_side_effects=True, vmem_limit_bytes=32 * 1024 * 1024
        ),
    )(
        *(
            pltpu.with_memory_space_constraint(array, pltpu.HBM)
            for array in (
                hidden_in,
                norm_gain.reshape(chunks, LANES),
                w_query,
                key_weight.T,
                value_weight.T,
                w_output,
                key_cache_units.reshape(slots, cache_cols),
                value_cache_units.reshape(slots, cache_cols),
                key_scale.reshape(blocks, GROUPS).T,
                value_block_scale.reshape(blocks, GROUPS).T,
            )
        ),
        lengths,
    )
    return out.reshape(1, width)


def solution(mesh):
    placed = (
        P(("gx", "gy"), None),
        P(),
        P("gx", "gy"),
        P("gx", "gy"),
        P("gx", "gy"),
        P("gx", "gy"),
        P(("gx", "gy"), None, None),
        P(("gx", "gy"), None, None),
        P(("gx", "gy"), None, None),
        P(("gx", "gy"), None, None),
        P(("gx", "gy")),
    )
    return jax.shard_map(
        functools.partial(body, mesh.shape["gx"], mesh.shape["gy"]),
        mesh=mesh,
        in_specs=placed,
        out_specs=P(("gx", "gy"), None),
        check_vma=False,
    )
```

```python
import functools
import math

import jax
import jax.numpy as jnp
from jax import lax
from jax.experimental import pallas as pl
from jax.experimental.pallas import tpu as pltpu
from jax.sharding import PartitionSpec as P

MESH = pl.DeviceIdType.MESH
F32 = jnp.float32
BF16 = jnp.bfloat16

GROUPS = 8
LANES = 128
ROPE_BASE = 500000.0
NORM_EPS = 1e-05
MASKED_SCORE = -1e30


def kernel(
    nz,
    ny,
    hidden_hbm,
    gain_hbm,
    wq_hbm,
    wk_hbm,
    wv_hbm,
    wo_hbm,
    keys_hbm,
    values_hbm,
    key_scale_hbm,
    value_scale_hbm,
    lengths,
    out_ref,
    hidden,
    gain,
    wq,
    wkv,
    wo,
    keys,
    values,
    wide,
    a_src,
    a_dst,
    spare,
    b_src,
    b_dst,
    heads_in,
    rows,
    queries,
    kscale,
    vscale,
    c_src,
    c_dst,
    d_src,
    d_dst,
    key_scale,
    value_scale,
    load_sem,
    send_core,
    recv_core,
    send_far,
    recv_far,
):
    gx = lax.axis_index("gx")
    gy = lax.axis_index("gy")
    z, core = gx // 2, lax.rem(gx, 2)
    other = 1 - core
    side = 4
    px, py = gy // side, lax.rem(gy, side)
    chips = nz * ny
    chip = z * ny + gy
    slots = keys.shape[0]
    blocks = slots // LANES

    key_cols = wk_hbm.shape[0]
    loads = [
        pltpu.make_async_copy(src, dst, load_sem.at[i])
        for i, (src, dst) in enumerate(
            (
                (hidden_hbm, hidden),
                (gain_hbm, gain),
                (wk_hbm, wkv.at[core, pl.ds(0, key_cols)]),
                (wv_hbm, wkv.at[core, pl.ds(key_cols, key_cols)]),
                (wq_hbm, wq.at[core]),
                (keys_hbm, keys),
                (values_hbm, values),
                (wo_hbm, wo.at[core]),
                (key_scale_hbm, key_scale),
                (value_scale_hbm, value_scale),
            )
        )
    ]
    loads[0].start()
    loads[1].start()

    steps = (0, 1, 2, 3)
    hops = (0, 1, 2, 1)
    along_z = [lax.rem(z + d, nz) for d in steps]
    along_x = [lax.rem(px + d, side) * side for d in steps]
    along_y = [lax.rem(py + d, side) for d in steps]

    def by_distance(layers):
        return sorted(
            ((a, b, c) for a in layers for b in steps for c in steps if (a, b, c) != (0, 0, 0)),
            key=lambda d: (-hops[d[0]] - hops[d[1]] - hops[d[2]], d),
        )

    def plane(d):
        return along_x[d[1]] + along_y[d[2]]

    barrier = pltpu.get_barrier_semaphore()

    for d in by_distance(steps):
        pl.semaphore_signal(
            barrier, inc=1, device_id=(along_z[d[0]] * 2 + core, plane(d)), device_id_type=MESH
        )
    pl.semaphore_signal(barrier, inc=1, device_id=(z * 2 + other, gy), device_id_type=MESH)

    for load in loads[8:] + loads[2:8]:
        load.start()

    def to_core(i, src, dst):
        return pltpu.make_async_remote_copy(
            src_ref=src,
            dst_ref=dst,
            send_sem=send_core.at[i],
            recv_sem=recv_core.at[i],
            device_id=(z * 2 + other, gy),
            device_id_type=MESH,
        )

    def to_chip(i, src, dst, tz, ty):
        return pltpu.make_async_remote_copy(
            src_ref=src,
            dst_ref=dst.at[chip],
            send_sem=send_far.at[i],
            recv_sem=recv_far.at[i],
            device_id=(tz * 2 + core, ty),
            device_id_type=MESH,
        )

    def to_all(i, src, dst):
        for d in by_distance(steps):
            tz, ty = along_z[d[0]], plane(d)
            to_chip(i, src(tz, ty), dst, tz, ty).start()

    def wait_all(sem, ref):
        most = ref.at[pl.ds(0, ref.shape[0] - 1)]
        pltpu.make_async_copy(most, most, sem).wait()

    loads[0].wait()
    row = hidden[...].astype(F32)
    for s in range(wide.shape[0]):
        wide[s : s + 1, :] = row[:, s * LANES : (s + 1) * LANES]
    loads[1].wait()
    x = wide[...]
    variance = jnp.sum(jnp.sum(x * x, axis=0, keepdims=True), axis=1, keepdims=True) * (
        1.0 / (x.shape[0] * LANES)
    )
    x = (x * lax.rsqrt(variance + NORM_EPS) * gain[...]).astype(BF16)
    a_src[...] = x.reshape(a_src.shape)

    pl.semaphore_wait(barrier, chips)

    to_all(0, lambda tz, ty: a_src.at[tz], a_dst)
    a_dst[chip] = a_src[z]

    shared = [
        to_core(0, wk_hbm, wkv.at[core, pl.ds(0, key_cols)]),
        to_core(1, wv_hbm, wkv.at[core, pl.ds(key_cols, key_cols)]),
        to_core(2, wq_hbm, wq.at[core]),
        to_core(3, wo_hbm, wo.at[core]),
    ]
    for share in shared:
        share.start()

    length = lengths[0]
    lane = lax.broadcasted_iota(jnp.int32, (1, LANES), 1)
    step = (lane % 64).astype(F32)
    angle = length.astype(F32) * jnp.exp(step * (-2.0 * math.log(ROPE_BASE) / LANES))
    inv_root = 1.0 / math.sqrt(LANES)

    cosine = jnp.cos(angle)
    sine = jnp.sin(angle)
    sine = jnp.where(lane < 64, -sine, sine)

    loads[8].wait()
    loads[9].wait()

    @pl.loop(0, blocks)
    def _(b):
        at = pl.ds(pl.multiple_of(b * LANES, LANES), LANES)
        for g in range(GROUPS):
            kscale[8 * g : 8 * g + 8, at] = jnp.full((8, LANES), key_scale[g, b] * inv_root, F32)
            vscale[8 * g : 8 * g + 8, at] = jnp.full((8, LANES), value_scale[g, b], F32)

    loads[2].wait()
    loads[3].wait()
    loads[4].wait()

    for share in shared[:3]:
        share.wait_recv()

    nt = (((1,), (1,)), ((), ()))

    def requests(arrived):
        spare[...] = arrived[...].astype(F32).reshape(spare.shape)
        chunks = [spare[pl.ds(s, chips, stride=16), :] for s in range(16)]
        return (
            jnp.concatenate(chunks[:8], axis=1).astype(BF16),
            jnp.concatenate(chunks[8:], axis=1).astype(BF16),
        )

    def product(low, high, weights):
        return jnp.dot(low, weights[0], preferred_element_type=F32) + jnp.dot(
            high, weights[1], preferred_element_type=F32
        )

    def product_nt(low, high, weights):
        return lax.dot_general(
            low, weights[0], nt, preferred_element_type=F32
        ) + lax.dot_general(high, weights[1], nt, preferred_element_type=F32)

    def reduce(i, parts, src, dst):
        at = 0
        for part in parts:
            for c in range(part.shape[1] // LANES):
                src[:, at, :] = part[:, c * LANES : (c + 1) * LANES]
                at += 1
        to_all(i, lambda tz, ty: src.at[tz * ny + ty], dst)
        dst[chip] = src[chip]
        wait_all(recv_far.at[i], dst)
        summed = dst[0:ny]
        for t in range(1, nz):
            summed = summed + dst[t * ny : (t + 1) * ny]
        return summed

    wait_all(recv_far.at[0], a_dst)
    low, high = requests(a_dst)
    summed = reduce(1, (product(low, high, wq), product_nt(low, high, wkv)), b_src, b_dst)
    heads_in[:, 0 : summed.shape[1], :] = summed.astype(BF16).astype(F32)

    per = wq.shape[2] // LANES
    for j in range(per):
        rows[pl.ds(j, ny, stride=per), :] = heads_in[:, j, :]
    both = heads_in[:, per, :]
    queries[0:ny, :] = both
    even = queries[pl.ds(0, ny // 2, stride=2), :]
    odd = queries[pl.ds(1, ny // 2, stride=2), :]
    front = lane < 64
    new_key = jnp.where(front, even, pltpu.roll(odd, 64, 1))
    new_value = jnp.where(front, pltpu.roll(even, 64, 1), odd)

    def rotate(v):
        return (v * cosine + pltpu.roll(v, 64, 1) * sine).astype(BF16).astype(F32)

    heads_in[0, :, :] = rotate(new_key)
    heads_in[1, :, :] = new_value
    queries[...] = rotate(rows[...])

    loads[5].wait()
    loads[6].wait()
    top = lax.broadcasted_iota(jnp.int32, (16, LANES), 0) < 8
    live = lax.broadcasted_iota(jnp.int32, (1, slots), 1) < length

    def score(p):
        cols = pl.ds(pl.multiple_of(2 * p * LANES, 2 * LANES), 2 * LANES)
        heads = pl.ds(pl.multiple_of(16 * p, 16), 16)
        q = queries[heads, :]
        spread_q = jnp.concatenate([jnp.where(top, q, 0.0), jnp.where(top, 0.0, q)], axis=1)
        scores = lax.dot_general(
            spread_q.astype(BF16), keys[:, cols], nt, preferred_element_type=F32
        )
        return jnp.where(live, scores * kscale[heads, :], MASKED_SCORE)

    def attend(p, scores):
        cols = pl.ds(pl.multiple_of(2 * p * LANES, 2 * LANES), 2 * LANES)
        heads = pl.ds(pl.multiple_of(16 * p, 16), 16)
        q = queries[heads, :]
        own_key = jnp.where(
            top, heads_in[0, pl.ds(2 * p, 1), :], heads_in[0, pl.ds(2 * p + 1, 1), :]
        )
        own_value = jnp.where(
            top, heads_in[1, pl.ds(2 * p, 1), :], heads_in[1, pl.ds(2 * p + 1, 1), :]
        )
        own_score = jnp.sum(q * own_key, axis=1, keepdims=True) * inv_root
        peak = jnp.maximum(jnp.max(scores, axis=1, keepdims=True), own_score)
        probs = jnp.exp(scores - peak)
        own_prob = jnp.exp(own_score - peak)
        total = jnp.sum(probs, axis=1, keepdims=True) + own_prob
        weighted = (probs * vscale[heads, :]).astype(BF16)
        mixed = jnp.dot(weighted, values[:, cols], preferred_element_type=F32)
        mixed = jnp.where(top, mixed[:, :LANES], mixed[:, LANES:])
        mixed = mixed + own_prob.astype(BF16).astype(F32) * own_value
        c_src[p] = (mixed / total).astype(BF16)

    def send_heads(a):
        p = along_z[a]
        for d in by_distance((a,)):
            to_chip(2, c_src.at[p], c_dst, p, plane(d)).start()

    order = (2, 1, 3, 0)
    every = [score(along_z[a]) for a in order]
    for k in range(nz):
        attend(along_z[order[k]], every[k])
        send_heads(order[k])

    c_dst[chip] = c_src[z]

    loads[7].wait()
    wait_all(recv_far.at[2], c_dst)
    shared[3].wait_recv()
    low, high = requests(c_dst)
    summed = reduce(3, (product(low, high, wo),), d_src, d_dst)
    for j in range(per):
        rows[pl.ds(j, ny, stride=per), :] = summed[:, j, :]
    out_ref[...] = (wide[...] + rows[...]).astype(BF16)

    for share in shared:
        share.wait_send()
    wait_all(send_far.at[0], a_dst)
    wait_all(send_far.at[1], b_dst)
    wait_all(send_far.at[2], c_dst)
    wait_all(send_far.at[3], d_dst)


def body(
    nx,
    ny,
    hidden_in,
    norm_gain,
    w_query,
    key_weight,
    value_weight,
    w_output,
    key_cache_units,
    value_cache_units,
    key_scale,
    value_block_scale,
    lengths,
):
    width = hidden_in.shape[1]
    chunks = width // LANES
    depth, query_cols = w_query.shape
    key_cols = key_weight.shape[1]
    slots, cache_cols = key_cache_units.shape[1:]
    blocks = key_scale.shape[1]
    cols = query_cols + 2 * key_cols
    nz = nx // 2
    chips = nz * ny
    hbm = pl.BlockSpec(memory_space=pltpu.HBM)
    vmem = pltpu.VMEM
    out = pl.pallas_call(
        functools.partial(kernel, nz, ny),
        out_shape=jax.ShapeDtypeStruct((chunks, LANES), BF16),
        in_specs=[hbm] * 10 + [pl.BlockSpec(memory_space=pltpu.SMEM)],
        out_specs=pl.BlockSpec(memory_space=pltpu.VMEM),
        scratch_shapes=[
            vmem((1, width), BF16),
            vmem((chunks, LANES), F32),
            vmem((2, depth, query_cols), BF16),
            vmem((2, 2 * key_cols, depth), BF16),
            vmem((2, depth, query_cols), BF16),
            vmem((slots, cache_cols), BF16),
            vmem((slots, cache_cols), BF16),
            vmem((chunks, LANES), F32),
            vmem((nz, 16, LANES), BF16),
            vmem((chips, 16, LANES), BF16),
            vmem((chips * 16, LANES), F32),
            vmem((chips, cols // LANES, LANES), F32),
            vmem((chips, cols // LANES, LANES), F32),
            vmem((ny, 8, LANES), F32),
            vmem((chunks, LANES), F32),
            vmem((chunks, LANES), F32),
            vmem((chunks, slots), F32),
            vmem((chunks, slots), F32),
            vmem((nz, 16, LANES), BF16),
            vmem((chips, 16, LANES), BF16),
            vmem((chips, query_cols // LANES, LANES), F32),
            vmem((chips, query_cols // LANES, LANES), F32),
            pltpu.SMEM((GROUPS, blocks), F32),
            pltpu.SMEM((GROUPS, blocks), F32),
            pltpu.SemaphoreType.DMA((10,)),
            pltpu.SemaphoreType.DMA((4,)),
            pltpu.SemaphoreType.DMA((4,)),
            pltpu.SemaphoreType.DMA((4,)),
            pltpu.SemaphoreType.DMA((4,)),
        ],
        compiler_params=pltpu.CompilerParams(
            collective_id=0, has_side_effects=True, vmem_limit_bytes=32 * 1024 * 1024
        ),
    )(
        *(
            pltpu.with_memory_space_constraint(array, pltpu.HBM)
            for array in (
                hidden_in,
                norm_gain.reshape(chunks, LANES),
                w_query,
                key_weight.T,
                value_weight.T,
                w_output,
                key_cache_units.reshape(slots, cache_cols),
                value_cache_units.reshape(slots, cache_cols),
                key_scale.reshape(blocks, GROUPS).T,
                value_block_scale.reshape(blocks, GROUPS).T,
            )
        ),
        lengths,
    )
    return out.reshape(1, width)


def solution(mesh):
    placed = (
        P(("gx", "gy"), None),
        P(),
        P("gx", "gy"),
        P("gx", "gy"),
        P("gx", "gy"),
        P("gx", "gy"),
        P(("gx", "gy"), None, None),
        P(("gx", "gy"), None, None),
        P(("gx", "gy"), None, None),
        P(("gx", "gy"), None, None),
        P(("gx", "gy")),
    )
    return jax.shard_map(
        functools.partial(body, mesh.shape["gx"], mesh.shape["gy"]),
        mesh=mesh,
        in_specs=placed,
        out_specs=P(("gx", "gy"), None),
        check_vma=False,
    )
```
